32 devices in a mesh: shard: 2 (over core), ctx: 4 (over z), tp: 4 (over y, x).
Axes of the slice: x: 2, y: 2, z: 4, core: 2. Of those that a mesh axis runs over, the one named last changes fastest.
Arguments:
- inputs: bfloat16 [2, 1024, 1152], P('shard', 'ctx'), may hold values from -6 to 6
- positions: int32 [2, 1024], P('shard', 'ctx'), may hold values from 0 to 1023, as said below
- cotangent: bfloat16 [2, 1024, 1152], P('shard', 'ctx'), may hold values from -6 to 6
- w_query: bfloat16 [1152, 1024], P(('shard', 'ctx'), 'tp'), may hold values from -0.1875 to 0.1875
- w_keyval: bfloat16 [1152, 512], P(('shard', 'ctx'), 'tp'), may hold values from -0.1875 to 0.1875
- w_out: bfloat16 [1152, 1024], P(('shard', 'ctx'), 'tp'), may hold values from -0.1875 to 0.1875
- w_gate: bfloat16 [1152, 6912], P(('shard', 'ctx'), 'tp'), may hold values from -0.1875 to 0.1875
- w_up: bfloat16 [1152, 6912], P(('shard', 'ctx'), 'tp'), may hold values from -0.1875 to 0.1875
- w_down: bfloat16 [1152, 6912], P(('shard', 'ctx'), 'tp'), may hold values from -0.078125 to 0.078125
- gain_input: float32 [1152], replicated, may hold values from 0.5 to 1.5
- gain_query: float32 [256], replicated, may hold values from 0.5 to 1.5
- gain_key: float32 [256], replicated, may hold values from 0.5 to 1.5
- gain_attn: float32 [1152], replicated, may hold values from 0.5 to 1.5
- gain_prefn: float32 [1152], replicated, may hold values from 0.5 to 1.5
- gain_postfn: float32 [1152], replicated, may hold values from 0.5 to 1.5
Outputs:
- block_out: float32 [2, 1024, 1152], P('shard', 'ctx')
- input_grad: float32 [2, 1024, 1152], P('shard', 'ctx')
- query_grad: float32 [1152, 1024], P(('shard', 'ctx'), 'tp')
- keyval_grad: float32 [1152, 512], P(('shard', 'ctx'), 'tp')
- output_grad: float32 [1152, 1024], P(('shard', 'ctx'), 'tp')
- gate_grad: float32 [1152, 6912], P(('shard', 'ctx'), 'tp')
- up_proj_grad: float32 [1152, 6912], P(('shard', 'ctx'), 'tp')
- down_grad: float32 [1152, 6912], P(('shard', 'ctx'), 'tp')
- gain_input_grad: float32 [1152], P(('shard', 'ctx'))
- gain_query_grad: float32 [256], P(('shard', 'ctx'))
- gain_key_grad: float32 [256], P(('shard', 'ctx'))
- gain_attn_grad: float32 [1152], P(('shard', 'ctx'))
- gain_prefn_grad: float32 [1152], P(('shard', 'ctx'))
- gain_postfn_grad: float32 [1152], P(('shard', 'ctx'))
The draws below stay inside these ranges and needn't reach their ends.
Inputs may be any that keep to these rules, and one draw needn't show every extreme that they name: Each aligned block of 128 rows of a sequence holds 128 consecutive positions in rising order, starting at a multiple of 128; the rows of one sequence hold every position from 0 to 1023 once.
All inputs are finite; a program needn't handle non-finite values.
Results may differ from the reference program's by a relative error of at most 0.025.
Values may be sent and summed in bfloat16 or wider, within the bound.
No kernel may reach another device: no remote copies, remote signals or barrier semaphores. Data moves between devices by JAX's collectives and lax.ppermute only.
A program may use at most 128 MiB of HBM per device.

```python
import math
import jax
import jax.numpy as jnp
from jax import lax

D = 1152
HEADS = 4
HD = 256
FF = 6912
SEQS = 2
LEN = 1024
GROUP = 128
N_CTX = 4


def draw_positions(key, part):
    keys = jax.random.split(jax.random.fold_in(key, 17), SEQS)
    orders = jax.vmap(lambda single: jax.random.permutation(single, 2 * N_CTX))(keys)
    offsets = jnp.arange(GROUP, dtype=jnp.int32)
    table = orders.astype(jnp.int32)[:, :, None] * GROUP + offsets[None, None, :]
    return table.reshape(SEQS, LEN).astype(jnp.int32)


def block_levels(rng, dims, cuts, low, largest):
    level = 1.0
    for position, shards_of in cuts:
        steps = jax.random.uniform(jax.random.fold_in(jax.random.fold_in(rng, 6), position), (shards_of,), jnp.float32, low / len(cuts), largest / len(cuts))
        level = level * jnp.repeat(jnp.exp(steps), dims[position] // shards_of).reshape((-1,) + (1,) * (len(dims) - 1 - position))
    return level


def centred(rng, extent, spread, bound, cuts=(), kind=jnp.bfloat16):
    values = spread * jax.random.normal(rng, extent, jnp.float32)
    if cuts:
        values = values * block_levels(rng, extent, cuts, -0.22, 0.18)
    return jnp.clip(values, -bound, bound).astype(kind)


def setup_inputs(seed: int = 0) -> dict:
    seeds = jax.random.split(jax.random.key(seed), 16)
    return {
        "inputs": centred(seeds[0], (SEQS, LEN, D), 1.0, 6.0, ((0, 2), (1, 4))),
        "positions": draw_positions(jax.random.fold_in(seeds[15], 71), 0),
        "cotangent": centred(seeds[2], (SEQS, LEN, D), 1.0, 6.0, ((0, 2), (1, 4))),
        "w_query": centred(seeds[3], (D, HEADS * HD), D ** -0.5, 0.1875, ((0, 8), (1, 4))),
        "w_keyval": centred(seeds[4], (D, 2 * HD), D ** -0.5, 0.1875, ((0, 8), (1, 4))),
        "w_out": centred(seeds[5], (D, HEADS * HD), (HEADS * HD) ** -0.5, 0.1875, ((0, 8), (1, 4))),
        "w_gate": centred(seeds[6], (D, FF), D ** -0.5, 0.1875, ((0, 8), (1, 4))),
        "w_up": centred(seeds[7], (D, FF), D ** -0.5, 0.1875, ((0, 8), (1, 4))),
        "w_down": centred(seeds[8], (D, FF), FF ** -0.5, 0.078125, ((0, 8), (1, 4))),
        "gain_input": jnp.clip(1.0 + 0.1 * jax.random.normal(seeds[9], (D,), jnp.float32), 0.5, 1.5),
        "gain_query": jnp.clip(1.0 + 0.1 * jax.random.normal(seeds[10], (HD,), jnp.float32), 0.5, 1.5),
        "gain_key": jnp.clip(1.0 + 0.1 * jax.random.normal(seeds[11], (HD,), jnp.float32), 0.5, 1.5),
        "gain_attn": jnp.clip(1.0 + 0.1 * jax.random.normal(seeds[12], (D,), jnp.float32), 0.5, 1.5),
        "gain_prefn": jnp.clip(1.0 + 0.1 * jax.random.normal(seeds[13], (D,), jnp.float32), 0.5, 1.5),
        "gain_postfn": jnp.clip(1.0 + 0.1 * jax.random.normal(seeds[14], (D,), jnp.float32), 0.5, 1.5),
    }


EPS = 1e-06
THETA = 1000000.0
SCALE = 0.0625
GELU_C = 0.7978845608028654

def rounded(values):
    return lax.optimization_barrier(values.astype(jnp.bfloat16)).astype(jnp.float32)

def rms_parts(values):
    factor = lax.rsqrt(lax.optimization_barrier(jnp.mean(values * values, axis=-1, keepdims=True)) + EPS)
    return (values * factor, factor)

def rms_back(upstream, normed, factor, gain):
    scaled = upstream * gain
    inner = lax.optimization_barrier(jnp.mean(scaled * normed, axis=-1, keepdims=True))
    return factor * (scaled - normed * inner)

def rotate_half(values):
    half = values.shape[-1] // 2
    return jnp.concatenate([-values[..., half:], values[..., :half]], axis=-1)

def rope_tables(tok_pos):
    half = HD // 2
    freq = THETA ** (-(jnp.arange(half, dtype=jnp.float32) * 2.0) / HD)
    angle = tok_pos.astype(jnp.float32)[:, None] * freq[None, :]
    cosine = jnp.concatenate([jnp.cos(angle), jnp.cos(angle)], axis=-1)
    sine = jnp.concatenate([jnp.sin(angle), jnp.sin(angle)], axis=-1)
    return (cosine, sine)

def rope(values, cosine, sine):
    return values * cosine + rotate_half(values) * sine

def rope_back(values, cosine, sine):
    return values * cosine - rotate_half(values * sine)

def gelu_parts(gate):
    inner = GELU_C * (gate + 0.044715 * gate * gate * gate)
    tangent = jnp.tanh(inner)
    value = 0.5 * gate * (1.0 + tangent)
    slope = 0.5 * (1.0 + tangent) + 0.5 * gate * (1.0 - tangent * tangent) * GELU_C * (1.0 + 3.0 * 0.044715 * gate * gate)
    return (value, slope)

def attention_forward(queries, keys, values, tok_pos):
    rows = queries.shape[0]
    block = math.gcd(rows, 512)
    count = rows // block
    query_blocks = queries.reshape(count, block, HEADS, HD)
    pos_blocks = tok_pos.reshape(count, block)
    key_float = keys.astype(jnp.float32)
    value_float = values.astype(jnp.float32)

    def one_block(pair):
        query_block, pos_block = pair
        scores = jnp.einsum('thd,kd->thk', query_block.astype(jnp.float32), key_float) * SCALE
        visible = tok_pos[None, None, :] <= pos_block[:, None, None]
        top = lax.optimization_barrier(jnp.max(jnp.where(visible, scores, -1e+30), axis=-1))
        weights = jnp.where(visible, jnp.exp(scores - top[..., None]), 0.0)
        total = lax.optimization_barrier(jnp.sum(weights, axis=-1))
        result = jnp.einsum('thk,kd->thd', rounded(weights), value_float) / total[..., None]
        return (result, top + jnp.log(total))
    results, lses = lax.map(one_block, (query_blocks, pos_blocks))
    return (results.reshape(rows, HEADS, HD), lses.reshape(rows, HEADS))

def attention_backward(queries, keys, values, tok_pos, lses, d_attn, delta):
    rows = queries.shape[0]
    block = math.gcd(rows, 512)
    count = rows // block
    key_float = keys.astype(jnp.float32)
    value_float = values.astype(jnp.float32)

    def one_block(carry, pieces):
        d_keys, d_values = carry
        query_block, pos_block, lse_block, grad_block, delta_block = pieces
        query_float = query_block.astype(jnp.float32)
        grad_float = grad_block.astype(jnp.float32)
        scores = jnp.einsum('thd,kd->thk', query_float, key_float) * SCALE
        visible = tok_pos[None, None, :] <= pos_block[:, None, None]
        probs = jnp.where(visible, jnp.exp(scores - lse_block[..., None]), 0.0)
        d_probs = jnp.einsum('thd,kd->thk', grad_float, value_float)
        d_scores = rounded(probs * (d_probs - delta_block[..., None]))
        d_query = jnp.einsum('thk,kd->thd', d_scores, key_float) * SCALE
        d_keys = d_keys + jnp.einsum('thk,thd->kd', d_scores, query_float) * SCALE
        d_values = d_values + jnp.einsum('thk,thd->kd', rounded(probs), grad_float)
        return ((d_keys, d_values), d_query)
    start = (jnp.zeros((rows, HD), jnp.float32), jnp.zeros((rows, HD), jnp.float32))
    pieces = (queries.reshape(count, block, HEADS, HD), tok_pos.reshape(count, block), lses.reshape(count, block, HEADS), d_attn.reshape(count, block, HEADS, HD), delta.reshape(count, block, HEADS))
    (d_keys, d_values), d_queries = lax.scan(one_block, start, pieces)
    return (d_queries.reshape(rows, HEADS, HD), d_keys, d_values)

def one_sequence(tokens, tok_pos, upstream_in, w_query, w_keyval, w_out, w_gate, w_up, w_down, gain_input, gain_query, gain_key, gain_attn, gain_prefn, gain_postfn):
    rows = tokens.shape[0]
    cosine, sine = rope_tables(tok_pos)
    x_float = tokens.astype(jnp.float32)
    x_hat, x_factor = rms_parts(x_float)
    normed_in = (x_hat * gain_input).astype(jnp.bfloat16)
    q_raw = jnp.dot(normed_in, w_query, preferred_element_type=jnp.float32).reshape(rows, HEADS, HD)
    kv_raw = jnp.dot(normed_in, w_keyval, preferred_element_type=jnp.float32).astype(jnp.bfloat16)
    k_hat, k_factor = rms_parts(kv_raw[:, :HD].astype(jnp.float32))
    keys = rope(k_hat * gain_key, cosine, sine).astype(jnp.bfloat16)
    values = kv_raw[:, HD:]
    q_hat, q_factor = rms_parts(q_raw)
    queries = rope(q_hat * gain_query, cosine[:, None, :], sine[:, None, :]).astype(jnp.bfloat16)
    attn_float, lses = attention_forward(queries, keys, values, tok_pos)
    attn = attn_float.astype(jnp.bfloat16).reshape(rows, HEADS * HD)
    o_proj = jnp.dot(attn, w_out.T, preferred_element_type=jnp.float32)
    o_hat, o_factor = rms_parts(o_proj)
    resid = x_float + o_hat * gain_attn
    h_hat, h_factor = rms_parts(resid)
    normed_ff = (h_hat * gain_prefn).astype(jnp.bfloat16)
    gate = jnp.dot(normed_ff, w_gate, preferred_element_type=jnp.float32)
    up_val = jnp.dot(normed_ff, w_up, preferred_element_type=jnp.float32)
    act, slope = gelu_parts(gate)
    mixed = (act * up_val).astype(jnp.bfloat16)
    f_sum = jnp.dot(mixed, w_down.T, preferred_element_type=jnp.float32)
    f_hat, f_factor = rms_parts(f_sum)
    block_out = resid + f_hat * gain_postfn
    upstream = upstream_in.astype(jnp.float32)
    grad_postfn = lax.optimization_barrier(jnp.sum(upstream * f_hat, axis=0))
    d_f = rms_back(upstream, f_hat, f_factor, gain_postfn).astype(jnp.bfloat16)
    grad_down = jnp.dot(d_f.T, mixed, preferred_element_type=jnp.float32)
    d_mixed = jnp.dot(d_f, w_down, preferred_element_type=jnp.float32)
    d_gate = (d_mixed * up_val * slope).astype(jnp.bfloat16)
    d_up = (d_mixed * act).astype(jnp.bfloat16)
    grad_gate = jnp.dot(normed_ff.T, d_gate, preferred_element_type=jnp.float32)
    grad_up = jnp.dot(normed_ff.T, d_up, preferred_element_type=jnp.float32)
    d_ff = jnp.dot(d_gate, w_gate.T, preferred_element_type=jnp.float32) + jnp.dot(d_up, w_up.T, preferred_element_type=jnp.float32)
    grad_prefn = lax.optimization_barrier(jnp.sum(d_ff * h_hat, axis=0))
    d_resid = upstream + rms_back(d_ff, h_hat, h_factor, gain_prefn)
    grad_attn = lax.optimization_barrier(jnp.sum(d_resid * o_hat, axis=0))
    d_o = rms_back(d_resid, o_hat, o_factor, gain_attn).astype(jnp.bfloat16)
    grad_out = jnp.dot(d_o.T, attn, preferred_element_type=jnp.float32)
    d_attn = jnp.dot(d_o, w_out, preferred_element_type=jnp.float32).astype(jnp.bfloat16).reshape(rows, HEADS, HD)
    delta = lax.optimization_barrier(jnp.sum(d_attn.astype(jnp.float32) * attn.reshape(rows, HEADS, HD).astype(jnp.float32), axis=-1))
    d_queries, d_keys, d_values = attention_backward(queries, keys, values, tok_pos, lses, d_attn, delta)
    d_knorm = rope_back(d_keys, cosine, sine)
    grad_key = lax.optimization_barrier(jnp.sum(d_knorm * k_hat, axis=0))
    d_kraw = rms_back(d_knorm, k_hat, k_factor, gain_key)
    d_kv = jnp.concatenate([d_kraw, d_values], axis=1).astype(jnp.bfloat16)
    d_qnorm = rope_back(d_queries, cosine[:, None, :], sine[:, None, :])
    grad_query = lax.optimization_barrier(jnp.sum(d_qnorm * q_hat, axis=(0, 1)))
    d_qraw = rms_back(d_qnorm, q_hat, q_factor, gain_query).astype(jnp.bfloat16).reshape(rows, HEADS * HD)
    grad_wq = jnp.dot(normed_in.T, d_qraw, preferred_element_type=jnp.float32)
    grad_wkv = jnp.dot(normed_in.T, d_kv, preferred_element_type=jnp.float32)
    d_in = jnp.dot(d_qraw, w_query.T, preferred_element_type=jnp.float32) + jnp.dot(d_kv, w_keyval.T, preferred_element_type=jnp.float32)
    grad_input = lax.optimization_barrier(jnp.sum(d_in * x_hat, axis=0))
    input_grad = d_resid + rms_back(d_in, x_hat, x_factor, gain_input)
    grads = (grad_wq, grad_wkv, grad_out, grad_gate, grad_up, grad_down, grad_input, grad_query, grad_key, grad_attn, grad_prefn, grad_postfn)
    return (block_out, input_grad, grads)

def reference(inputs, positions, cotangent, w_query, w_keyval, w_out, w_gate, w_up, w_down, gain_input, gain_query, gain_key, gain_attn, gain_prefn, gain_postfn):
    outputs = []
    in_grads = []
    grad_lists = []
    for index in range(SEQS):
        block_out, input_grad, grads = one_sequence(inputs[index], positions[index], cotangent[index], w_query, w_keyval, w_out, w_gate, w_up, w_down, gain_input, gain_query, gain_key, gain_attn, gain_prefn, gain_postfn)
        outputs.append(block_out)
        in_grads.append(input_grad)
        grad_lists.append(grads)
    totals = [sum((member[place] for member in grad_lists)) for place in range(12)]
    return (jnp.stack(outputs), jnp.stack(in_grads), totals[0], totals[1], totals[2], totals[3], totals[4], totals[5], totals[6], totals[7], totals[8], totals[9], totals[10], totals[11])
```

```python
import jax
import jax.numpy as jnp
from jax import lax
from jax.sharding import PartitionSpec as P

HD = 256
EPS = 1e-06
THETA = 1000000.0
SCALE = 0.0625
GELU_C = 0.7978845608028654
BF = jnp.bfloat16
F32 = jnp.float32


def rms_parts(values):
    factor = lax.rsqrt(jnp.mean(values * values, axis=-1, keepdims=True) + EPS)
    return (values * factor, factor)


def rms_back(upstream, normed, factor, gain):
    scaled = upstream * gain
    inner = jnp.mean(scaled * normed, axis=-1, keepdims=True)
    return factor * (scaled - normed * inner)


def rotate_half(values):
    half = values.shape[-1] // 2
    return jnp.concatenate([-values[..., half:], values[..., :half]], axis=-1)


def rope_tables(tok_pos):
    half = HD // 2
    freq = THETA ** (-(jnp.arange(half, dtype=F32) * 2.0) / HD)
    angle = tok_pos.astype(F32)[:, None] * freq[None, :]
    cosine = jnp.cos(angle)
    sine = jnp.sin(angle)
    return (jnp.concatenate([cosine, cosine], axis=-1), jnp.concatenate([sine, sine], axis=-1))


def rope(values, cosine, sine):
    return values * cosine + rotate_half(values) * sine


def rope_back(values, cosine, sine):
    return values * cosine - rotate_half(values * sine)


def gelu_parts(gate):
    inner = GELU_C * (gate + 0.044715 * gate * gate * gate)
    tangent = jnp.tanh(inner)
    value = 0.5 * gate * (1.0 + tangent)
    slope = 0.5 * (1.0 + tangent) + 0.5 * gate * (1.0 - tangent * tangent) * GELU_C * (
        1.0 + 3.0 * 0.044715 * gate * gate
    )
    return (value, slope)


def dot(a, b):
    return jnp.dot(a, b, preferred_element_type=F32)


def dot_nt(a, b):
    return jnp.einsum("ik,jk->ij", a, b, preferred_element_type=F32)


def dot_tn(a, b):
    return jnp.einsum("ki,kj->ij", a, b, preferred_element_type=F32)


def xor_perm(size, bit):
    return [(i, i ^ bit) for i in range(size)]


def bits_of(size):
    out = []
    bit = size >> 1
    while bit:
        out.append(bit)
        bit >>= 1
    return out


def xor_swap(x, axis, bit):
    return lax.ppermute(x, axis, xor_perm(lax.axis_size(axis), bit))


def gather_pieces(x):
    pieces = [x]
    for bit in bits_of(lax.axis_size("ctx")):
        pieces = pieces + [xor_swap(p, "ctx", bit) for p in pieces]
    return pieces


def gather_rows(x):
    mine = jnp.concatenate(gather_pieces(x), axis=0)
    other = xor_swap(mine, "shard", 1)
    return jnp.concatenate([mine, other], axis=0)


def scatter_ctx(x):
    for bit in reversed(bits_of(lax.axis_size("ctx"))):
        half = x.shape[0] // 2
        x = x[:half] + xor_swap(x[half:].astype(BF), "ctx", bit).astype(F32)
    return x


def scatter_rows(x):
    half = x.shape[0] // 2
    x = x[:half] + xor_swap(x[half:].astype(BF), "shard", 1).astype(F32)
    return scatter_ctx(x)


def relative_blocks(x, axis, inverse=False):
    n = lax.axis_size("ctx")
    bits = bits_of(n)
    order = [0]
    for bit in bits:
        order = order + [k ^ bit for k in order]
    total = 2 * n
    block = x.shape[axis] // total
    me = lax.axis_index("ctx")
    shard = lax.axis_index("shard")

    def cond_swap(y, flag, span):
        parts = []
        for start in range(0, total, 2 * span):
            a = lax.slice_in_dim(y, start * block, (start + span) * block, axis=axis)
            b = lax.slice_in_dim(y, (start + span) * block, (start + 2 * span) * block, axis=axis)
            parts += [b, a]
        return jnp.where(flag, jnp.concatenate(parts, axis=axis), y)

    def static(y, where):
        parts = []
        for u in range(2):
            for k in where:
                base = u * n + k
                parts.append(lax.slice_in_dim(y, base * block, (base + 1) * block, axis=axis))
        return jnp.concatenate(parts, axis=axis)

    def swaps(y):
        y = cond_swap(y, shard == 1, n)
        for bit in bits:
            y = cond_swap(y, (me & bit) != 0, bit)
        return y

    if inverse:
        back = [order.index(k) for k in range(n)]
        return swaps(static(x, back))
    return static(swaps(x), order)


def all_reduce_tp(part):
    n = lax.axis_size("tp")
    rows = part.shape[0]
    sent = part.astype(BF).reshape((n, rows // n) + part.shape[1:])
    got = lax.all_to_all(sent, "tp", 0, 0)
    summed = jnp.sum(got.astype(F32), axis=0).astype(BF)
    return lax.all_gather(summed, "tp", axis=0, tiled=True).astype(F32)


def per_device(
    inputs,
    positions,
    cotangent,
    w_query,
    w_keyval,
    w_out,
    w_gate,
    w_up,
    w_down,
    gain_input,
    gain_query,
    gain_key,
    gain_attn,
    gain_prefn,
    gain_postfn,
):
    tok_pos = positions[0]
    n_ctx = lax.axis_size("ctx")
    n_tp = lax.axis_size("tp")
    count = inputs.shape[1]
    qc = w_query.shape[1]
    kc = w_keyval.shape[1]
    heads = qc // HD
    ff = w_gate.shape[1]

    pos_all = jnp.concatenate(gather_pieces(tok_pos), axis=0)
    wqkv = gather_rows(jnp.concatenate([w_query, w_keyval], axis=1))
    wo = gather_rows(w_out)
    wgu = gather_rows(jnp.concatenate([w_gate, w_up], axis=1))
    wd = gather_rows(w_down)

    both = relative_blocks(jnp.concatenate([inputs[0], cotangent[0]], axis=0), 1)
    gains = relative_blocks(jnp.stack([gain_input, gain_attn, gain_prefn, gain_postfn]), 1)
    g_in, g_attn, g_pre, g_post = gains[0], gains[1], gains[2], gains[3]
    x_float = both[:count].astype(F32)
    upstream = both[count:].astype(F32)

    cos_all, sin_all = rope_tables(pos_all)
    cosine, sine = cos_all[:count], sin_all[:count]
    x_hat, x_factor = rms_parts(x_float)
    normed_in = (x_hat * g_in).astype(BF)
    qkv = dot(normed_in, wqkv)
    q_raw = qkv[:, :qc].reshape(count, heads, HD)
    kv_part = qkv[:, qc:].astype(BF)

    kv_cols = jnp.concatenate(gather_pieces(kv_part), axis=0)
    spread = jnp.broadcast_to(kv_cols[None], (n_tp,) + kv_cols.shape)
    kv_stack = lax.all_to_all(spread, "tp", 0, 0)
    kv_raw = jnp.concatenate([kv_stack[i] for i in range(n_tp)], axis=1)
    k_hat_all, k_factor_all = rms_parts(kv_raw[:, :HD].astype(F32))
    keys = rope(k_hat_all * gain_key, cos_all, sin_all).astype(BF)
    values = kv_raw[:, HD:]

    q_hat, q_factor = rms_parts(q_raw)
    queries = rope(q_hat * gain_query, cosine[:, None, :], sine[:, None, :]).astype(BF)
    visible = pos_all[None, :] <= tok_pos[:, None]

    scores, probs_n, lses, outs = [], [], [], []
    for h in range(heads):
        s = dot_nt(queries[:, h], keys) * SCALE
        s = jnp.where(visible, s, -1e30)
        top = jnp.max(s, axis=-1, keepdims=True)
        w = jnp.exp(s - top)
        tot = jnp.sum(w, axis=-1, keepdims=True)
        outs.append((dot(w.astype(BF), values) / tot).astype(BF))
        lses.append(top + jnp.log(tot))
        scores.append(s)
    attn = jnp.concatenate(outs, axis=1)

    o_proj = all_reduce_tp(dot_nt(attn, wo))
    o_hat, o_factor = rms_parts(o_proj)
    resid = x_float + o_hat * g_attn
    h_hat, h_factor = rms_parts(resid)
    normed_ff = (h_hat * g_pre).astype(BF)
    gate_up = dot(normed_ff, wgu)
    gate, up_val = gate_up[:, :ff], gate_up[:, ff:]
    act, slope = gelu_parts(gate)
    mixed = (act * up_val).astype(BF)
    f_sum = all_reduce_tp(dot_nt(mixed, wd))
    f_hat, f_factor = rms_parts(f_sum)
    block_out = relative_blocks(resid + f_hat * g_post, 1, inverse=True)

    grad_postfn = jnp.sum(upstream * f_hat, axis=0)
    d_f = rms_back(upstream, f_hat, f_factor, g_post).astype(BF)
    grad_down = scatter_rows(dot_tn(d_f, mixed))
    d_mixed = dot(d_f, wd)
    d_gate = (d_mixed * up_val * slope).astype(BF)
    d_up = (d_mixed * act).astype(BF)
    grad_gate = scatter_rows(dot_tn(normed_ff, d_gate))
    grad_up = scatter_rows(dot_tn(normed_ff, d_up))
    d_gu = jnp.concatenate([d_gate, d_up], axis=1)
    d_ff = all_reduce_tp(dot_nt(d_gu, wgu))
    grad_prefn = jnp.sum(d_ff * h_hat, axis=0)
    d_resid = upstream + rms_back(d_ff, h_hat, h_factor, g_pre)
    grad_attn = jnp.sum(d_resid * o_hat, axis=0)
    d_o = rms_back(d_resid, o_hat, o_factor, g_attn).astype(BF)
    grad_out = scatter_rows(dot_tn(d_o, attn))
    d_attn = dot(d_o, wo).astype(BF)
    delta = jnp.sum(
        (d_attn.astype(F32) * attn.astype(F32)).reshape(count, heads, HD), axis=-1, keepdims=True
    )

    d_keys = jnp.zeros(keys.shape, F32)
    d_values = jnp.zeros(values.shape, F32)
    d_queries = []
    for h in range(heads):
        dah = d_attn[:, h * HD : (h + 1) * HD]
        probs = jnp.exp(scores[h] - lses[h])
        d_probs = dot_nt(dah, values)
        d_scores = (probs * (d_probs - delta[:, h])).astype(BF)
        d_queries.append(dot(d_scores, keys))
        d_keys = d_keys + dot_tn(d_scores, queries[:, h])
        d_values = d_values + dot_tn(probs.astype(BF), dah)

    quarter = count // n_tp
    dkv = jnp.concatenate([d_keys, d_values], axis=1).astype(BF)
    dkv = dkv.reshape(n_ctx, n_tp, quarter, 2 * HD).transpose(1, 0, 2, 3)
    dkv = lax.all_to_all(dkv, "tp", 0, 0)
    dkv = jnp.sum(dkv.astype(F32), axis=0).reshape(n_ctx * quarter, 2 * HD)
    dkv = scatter_ctx(dkv)
    first = lax.axis_index("tp") * quarter
    cos_q = lax.dynamic_slice_in_dim(cosine, first, quarter, 0)
    sin_q = lax.dynamic_slice_in_dim(sine, first, quarter, 0)
    khat_q = lax.dynamic_slice_in_dim(k_hat_all[:count], first, quarter, 0)
    kfac_q = lax.dynamic_slice_in_dim(k_factor_all[:count], first, quarter, 0)
    d_knorm = rope_back(dkv[:, :HD] * SCALE, cos_q, sin_q)
    grad_key_part = jnp.sum(d_knorm * khat_q, axis=0)
    d_kraw = rms_back(d_knorm, khat_q, kfac_q, gain_key)
    dkv_raw = jnp.concatenate([d_kraw, dkv[:, HD:]], axis=1).astype(BF)

    d_qnorm = rope_back(
        jnp.stack(d_queries, axis=1) * SCALE, cosine[:, None, :], sine[:, None, :]
    )
    grad_query_part = jnp.sum(d_qnorm * q_hat, axis=(0, 1))
    d_qraw = rms_back(d_qnorm, q_hat, q_factor, gain_query).astype(BF).reshape(count, qc)

    tail = jnp.concatenate([grad_query_part, grad_key_part])[None].astype(BF)
    tail = jnp.concatenate([tail, jnp.zeros((15, 2 * HD), BF)], axis=0)
    dkv_all = lax.all_gather(jnp.concatenate([dkv_raw, tail], axis=0), "tp", axis=0)
    dkv_full = dkv_all[:, :quarter].reshape(count, 2 * HD)
    gain_sums = jnp.sum(dkv_all[:, quarter].astype(F32), axis=0)
    dkv_cols = lax.dynamic_slice_in_dim(dkv_full, lax.axis_index("tp") * kc, kc, 1)
    d_qkv = jnp.concatenate([d_qraw, dkv_cols], axis=1)
    grad_qkv = scatter_rows(dot_tn(normed_in, d_qkv))
    d_in = all_reduce_tp(dot_nt(d_qkv, wqkv))
    grad_input = jnp.sum(d_in * x_hat, axis=0)
    input_grad = relative_blocks(
        d_resid + rms_back(d_in, x_hat, x_factor, g_in), 1, inverse=True
    )

    blocks = 2 * n_ctx
    wide = jnp.stack([grad_input, grad_attn, grad_prefn, grad_postfn]).reshape(4, blocks, -1)
    wide = wide.transpose(1, 0, 2).reshape(blocks, -1)
    narrow = relative_blocks(gain_sums.reshape(2, HD), 1).reshape(2, blocks, -1)
    narrow = narrow.transpose(1, 0, 2).reshape(blocks, -1)
    mine = scatter_rows(jnp.concatenate([wide, narrow], axis=1))[0]
    width = grad_input.shape[0] // blocks
    small = HD // blocks
    base = 4 * width
    return (
        block_out[None],
        input_grad[None],
        grad_qkv[:, :qc],
        grad_qkv[:, qc:],
        grad_out,
        grad_gate,
        grad_up,
        grad_down,
        mine[:width],
        mine[base : base + small],
        mine[base + small :],
        mine[width : 2 * width],
        mine[2 * width : 3 * width],
        mine[3 * width : 4 * width],
    )


def solution(mesh):
    rows = P(("shard", "ctx"), "tp")
    tokens = P("shard", "ctx", None)
    gain = P(("shard", "ctx"))
    return jax.shard_map(
        per_device,
        mesh=mesh,
        in_specs=(tokens, P("shard", "ctx"), tokens) + (rows,) * 6 + (P(),) * 6,
        out_specs=(tokens, tokens) + (rows,) * 6 + (gain,) * 6,
        check_vma=False,
    )
```

```python
import jax
import jax.numpy as jnp
from jax import lax
from jax.experimental import pallas as pl
from jax.experimental.pallas import tpu as pltpu
from jax.sharding import PartitionSpec as P

HD = 256
EPS = 1e-06
THETA = 1000000.0
SCALE = 0.0625
GELU_C = 0.7978845608028654
BF = jnp.bfloat16
F32 = jnp.float32


def rms_parts(values):
    factor = lax.rsqrt(jnp.mean(values * values, axis=-1, keepdims=True) + EPS)
    return (values * factor, factor)


def rms_back(upstream, normed, factor, gain):
    scaled = upstream * gain
    inner = jnp.mean(scaled * normed, axis=-1, keepdims=True)
    return factor * (scaled - normed * inner)


def rotate_half(values):
    half = values.shape[-1] // 2
    return jnp.concatenate([-values[..., half:], values[..., :half]], axis=-1)


def rope_tables(tok_pos):
    half = HD // 2
    freq = THETA ** (-(jnp.arange(half, dtype=F32) * 2.0) / HD)
    angle = tok_pos.astype(F32)[:, None] * freq[None, :]
    cosine = jnp.cos(angle)
    sine = jnp.sin(angle)
    return (jnp.concatenate([cosine, cosine], axis=-1), jnp.concatenate([sine, sine], axis=-1))


def rope(values, cosine, sine):
    return values * cosine + rotate_half(values) * sine


def rope_back(values, cosine, sine):
    return values * cosine - rotate_half(values * sine)


def gelu_parts(gate):
    inner = GELU_C * (gate + 0.044715 * gate * gate * gate)
    tangent = jnp.tanh(inner)
    value = 0.5 * gate * (1.0 + tangent)
    slope = 0.5 * (1.0 + tangent) + 0.5 * gate * (1.0 - tangent * tangent) * GELU_C * (
        1.0 + 3.0 * 0.044715 * gate * gate
    )
    return (value, slope)


def dot(a, b):
    return jnp.dot(a, b, preferred_element_type=F32)


def dot_nt(a, b):
    return jnp.einsum("ik,jk->ij", a, b, preferred_element_type=F32)


def dot_tn(a, b):
    return jnp.einsum("ki,kj->ij", a, b, preferred_element_type=F32)


def xor_swap(x, axis, bit):
    size = lax.axis_size(axis)
    return lax.ppermute(x, axis, [(i, i ^ bit) for i in range(size)])


def bits_of(size):
    out = []
    bit = size >> 1
    while bit:
        out.append(bit)
        bit >>= 1
    return out


def xor_order(size):
    order = [0]
    for bit in bits_of(size):
        order = order + [k ^ bit for k in order]
    return order


def gather_doubling(x):
    pieces = [x]
    for bit in bits_of(lax.axis_size("ctx")):
        pieces = pieces + [xor_swap(p, "ctx", bit) for p in pieces]
    return pieces


def gather_direct(x):
    n = lax.axis_size("ctx")
    if n > 4:
        return gather_doubling(x)
    return [x] + [xor_swap(x, "ctx", k) for k in xor_order(n)[1:]]


def with_other_core(pieces):
    return pieces + [xor_swap(p, "shard", 1) for p in pieces]


def natural_index():
    n = lax.axis_size("ctx")
    me = lax.axis_index("ctx")
    shard = lax.axis_index("shard")
    order = jnp.array(xor_order(n), jnp.int32)
    mine = jnp.bitwise_xor(order, me)
    return jnp.concatenate([shard * n + mine, (1 - shard) * n + mine]).astype(jnp.int32)


def in_order(pieces, index):
    rows = pieces[0].shape[0]
    if rows % 16 == 0:
        return pieces
    whole = jnp.zeros((rows * len(pieces),) + pieces[0].shape[1:], pieces[0].dtype)
    for j, piece in enumerate(pieces):
        whole = lax.dynamic_update_slice_in_dim(whole, piece, index[j] * rows, 0)
    return [whole]


def load_pieces(index_ref, refs, target, sems, lanes=None):
    rows = target.shape[0] // len(refs)
    copies = []
    for j, ref in enumerate(refs):
        if len(refs) == 1:
            where = target
        else:
            start = pl.multiple_of(index_ref[j] * rows, 16)
            where = target.at[pl.ds(start, rows)]
        source = ref
        if ref.shape[0] != rows or lanes is not None:
            source = ref.at[pl.ds(0, rows), lanes if lanes is not None else slice(None)]
        copy = pltpu.make_async_copy(source, where, sems.at[j])
        copy.start()
        copies.append(copy)
    return copies


def vmem():
    return pl.BlockSpec(memory_space=pltpu.VMEM)


def smem():
    return pl.BlockSpec(memory_space=pltpu.SMEM)


def anywhere():
    return pl.BlockSpec(memory_space=pl.ANY)


def spans(total, step):
    return [(at, min(step, total - at)) for at in range(0, total, step)]


PARAMS = pltpu.CompilerParams(vmem_limit_bytes=56 * 1024 * 1024)


def qkv_kernel(tokens, gain, index, pieces, qkv_cols):
    rows, width = tokens.shape
    count = len(pieces)
    out_cols = pieces[0].shape[1] - qkv_cols

    def body(index_ref, x_ref, g_ref, *refs):
        ins = refs[:count]
        a_ref, qkv_ref, wq_ref, wo_ref, sem_a, sem_b = refs[count:]
        copies = load_pieces(index_ref, ins, wq_ref, sem_a, pl.ds(0, qkv_cols))
        copies += load_pieces(index_ref, ins, wo_ref, sem_b, pl.ds(qkv_cols, out_cols))
        x = x_ref[...].astype(F32)
        hat, _ = rms_parts(x)
        a = (hat * g_ref[...]).astype(BF)
        a_ref[...] = a
        for copy in copies:
            copy.wait()
        qkv_ref[...] = dot(a, wq_ref[...])

    return pl.pallas_call(
        body,
        out_shape=(
            jax.ShapeDtypeStruct((rows, width), BF),
            jax.ShapeDtypeStruct((rows, qkv_cols), F32),
            jax.ShapeDtypeStruct((width, qkv_cols), BF),
            jax.ShapeDtypeStruct((width, out_cols), BF),
        ),
        in_specs=[smem(), vmem(), vmem()] + [anywhere()] * count,
        out_specs=(vmem(),) * 4,
        scratch_shapes=[pltpu.SemaphoreType.DMA((count,))] * 2,
        compiler_params=PARAMS,
        name="qkv_kernel",
    )(index, tokens, gain[None], *pieces)


def ff_forward(o_proj, tokens, g_attn, g_pre, index, gate_pieces, up_pieces):
    rows, width = tokens.shape
    count = len(gate_pieces)
    ff = gate_pieces[0].shape[1]

    def body(index_ref, o_ref, x_ref, ga_ref, gp_ref, *refs):
        gates, ups = refs[:count], refs[count : 2 * count]
        h1_ref, b_ref, mix_ref, p1_ref, p2_ref, wg, wu, sem_g, sem_u = refs[2 * count :]
        copies = load_pieces(index_ref, gates, wg, sem_g)
        copies += load_pieces(index_ref, ups, wu, sem_u)
        o_hat, _ = rms_parts(o_ref[...].astype(F32))
        h1 = x_ref[...].astype(F32) + o_hat * ga_ref[...]
        h1_ref[...] = h1
        h_hat, _ = rms_parts(h1)
        b_ref[...] = (h_hat * gp_ref[...]).astype(BF)
        for copy in copies:
            copy.wait()

        def chunk(lanes):
            b = b_ref[...]
            gate = dot(b, wg[:, lanes])
            up = dot(b, wu[:, lanes])
            act, slope = gelu_parts(gate)
            mix_ref[:, lanes] = (act * up).astype(BF)
            p1_ref[:, lanes] = (up * slope).astype(BF)
            p2_ref[:, lanes] = act.astype(BF)

        whole = ff // 256

        @pl.loop(0, whole)
        def _(c):
            chunk(pl.ds(pl.multiple_of(c * 256, 256), 256))

        if ff % 256:
            chunk(pl.ds(whole * 256, ff % 256))

    wide = jax.ShapeDtypeStruct((rows, ff), BF)
    return pl.pallas_call(
        body,
        out_shape=(
            jax.ShapeDtypeStruct((rows, width), F32),
            jax.ShapeDtypeStruct((rows, width), BF),
            wide,
            wide,
            wide,
        ),
        in_specs=[smem()] + [vmem()] * 4 + [anywhere()] * (2 * count),
        out_specs=(vmem(),) * 5,
        scratch_shapes=[
            pltpu.VMEM((width, ff), BF),
            pltpu.VMEM((width, ff), BF),
            pltpu.SemaphoreType.DMA((count,)),
            pltpu.SemaphoreType.DMA((count,)),
        ],
        compiler_params=PARAMS,
        name="ff_forward",
    )(index, o_proj, tokens, g_attn[None], g_pre[None], *gate_pieces, *up_pieces)


def ff_down(mixed, index, pieces, width):
    rows, ff = mixed.shape
    count = len(pieces)

    def body(index_ref, mix_ref, *refs):
        ins = refs[:count]
        f_ref, wd, sems = refs[count:]
        for copy in load_pieces(index_ref, ins, wd, sems):
            copy.wait()
        for at, size in spans(width, 384):
            f_ref[:, at : at + size] = dot_nt(mix_ref[...], wd[at : at + size, :]).astype(BF)

    return pl.pallas_call(
        body,
        out_shape=jax.ShapeDtypeStruct((rows, width), BF),
        in_specs=[smem(), vmem()] + [anywhere()] * count,
        out_specs=vmem(),
        scratch_shapes=[pltpu.VMEM((width, ff), BF), pltpu.SemaphoreType.DMA((count,))],
        compiler_params=PARAMS,
        name="ff_down",
    )(index, mixed, *pieces)


def ff_backward(f_sum, h1, cot, g_post, p1, p2, index, gate_pieces, up_pieces, down_pieces):
    rows, width = h1.shape
    ff = p1.shape[1]
    count = len(gate_pieces)

    def body(index_ref, f_ref, h1_ref, cot_ref, gp_ref, p1_ref, p2_ref, *refs):
        gates, ups, downs = refs[:count], refs[count : 2 * count], refs[2 * count : 3 * count]
        (out_ref, df_ref, gpost_ref, dg_ref, du_ref, dff_ref, wg, wu, wd, sem_g, sem_u, sem_d) = refs[
            3 * count :
        ]
        copies_d = load_pieces(index_ref, downs, wd, sem_d)
        copies = load_pieces(index_ref, gates, wg, sem_g)
        copies += load_pieces(index_ref, ups, wu, sem_u)
        f_hat, factor = rms_parts(f_ref[...].astype(F32))
        gain = gp_ref[...]
        out_ref[...] = h1_ref[...] + f_hat * gain
        up_stream = cot_ref[...].astype(F32)
        gpost_ref[...] = jnp.sum(up_stream * f_hat, axis=0, keepdims=True)
        df_ref[...] = rms_back(up_stream, f_hat, factor, gain).astype(BF)
        for copy in copies_d:
            copy.wait()

        def chunk(lanes):
            d_mixed = dot(df_ref[...], wd[:, lanes])
            dg_ref[:, lanes] = (d_mixed * p1_ref[:, lanes].astype(F32)).astype(BF)
            du_ref[:, lanes] = (d_mixed * p2_ref[:, lanes].astype(F32)).astype(BF)

        whole = ff // 256

        @pl.loop(0, whole)
        def _(c):
            chunk(pl.ds(pl.multiple_of(c * 256, 256), 256))

        if ff % 256:
            chunk(pl.ds(whole * 256, ff % 256))
        for copy in copies:
            copy.wait()
        for at, size in spans(width, 384):
            dff_ref[:, at : at + size] = (
                dot_nt(dg_ref[...], wg[at : at + size, :]) + dot_nt(du_ref[...], wu[at : at + size, :])
            ).astype(BF)

    return pl.pallas_call(
        body,
        out_shape=(
            jax.ShapeDtypeStruct((rows, width), F32),
            jax.ShapeDtypeStruct((rows, width), BF),
            jax.ShapeDtypeStruct((1, width), F32),
            jax.ShapeDtypeStruct((rows, ff), BF),
            jax.ShapeDtypeStruct((rows, ff), BF),
            jax.ShapeDtypeStruct((rows, width), BF),
        ),
        in_specs=[smem()] + [vmem()] * 6 + [anywhere()] * (3 * count),
        out_specs=(vmem(),) * 6,
        scratch_shapes=[pltpu.VMEM((width, ff), BF)] * 3 + [pltpu.SemaphoreType.DMA((count,))] * 3,
        compiler_params=PARAMS,
        name="ff_backward",
    )(index, f_sum, h1, cot, g_post[None], p1, p2, *gate_pieces, *up_pieces, *down_pieces)


def weight_grads(index, pairs, name):
    blocks = index.shape[0]
    half = blocks // 2
    rows, width = pairs[0][0].shape
    size = width // blocks
    cols = [right.shape[1] for _, right in pairs]
    count = len(pairs)
    lefts = []
    for left, _ in pairs:
        if not any(left is seen for seen in lefts):
            lefts.append(left)
    place = [next(i for i, seen in enumerate(lefts) if left is seen) for left, _ in pairs]
    turned = [left.T.reshape(blocks, size, rows) for left in lefts]

    def body(index_ref, *refs):
        ins, rights, outs = refs[: len(lefts)], refs[len(lefts) : len(lefts) + count], refs[len(lefts) + count :]
        step = pl.program_id(0)
        for p in range(count):
            result = dot(ins[place[p]][0], rights[p][...]).astype(BF)

            @pl.when(step < half)
            def _():
                outs[2 * p][0] = result

            @pl.when(step >= half)
            def _():
                outs[2 * p + 1][0] = result

    out_specs, out_shape = [], []
    for p in range(count):
        shape = (half, size, cols[p])
        out_shape += [jax.ShapeDtypeStruct(shape, BF)] * 2
        out_specs += [
            pl.BlockSpec((1, size, cols[p]), lambda j, ix: (jnp.minimum(j, half - 1), 0, 0)),
            pl.BlockSpec((1, size, cols[p]), lambda j, ix: (jnp.maximum(j - half, 0), 0, 0)),
        ]
    outs = pl.pallas_call(
        body,
        grid_spec=pltpu.PrefetchScalarGridSpec(
            num_scalar_prefetch=1,
            grid=(blocks,),
            in_specs=[pl.BlockSpec((1, size, rows), lambda j, ix: (ix[j], 0, 0))] * len(lefts)
            + [pl.BlockSpec((rows, c), lambda j, ix: (0, 0)) for c in cols],
            out_specs=out_specs,
        ),
        out_shape=out_shape,
        compiler_params=PARAMS,
        name=name,
    )(index, *turned, *[right for _, right in pairs])
    return [(outs[2 * p], outs[2 * p + 1]) for p in range(count)]


def scatter_ctx(x):
    bits = bits_of(lax.axis_size("ctx"))
    for place, bit in enumerate(reversed(bits)):
        half = x.shape[0] // 2
        got = xor_swap(x[half:].astype(BF), "ctx", bit)
        x = x[:half].astype(F32) + got.astype(F32)
        if place + 1 < len(bits):
            x = x.astype(BF)
    return x


def scatter_pair(keep, send):
    got = xor_swap(send, "shard", 1)
    bits = bits_of(lax.axis_size("ctx"))
    half = keep.shape[0] // 2
    low = keep[:half].astype(F32) + got[:half].astype(F32)
    high = (keep[half:].astype(F32) + got[half:].astype(F32)).astype(BF)
    for place, bit in enumerate(reversed(bits)):
        got = xor_swap(high, "ctx", bit)
        if place + 1 == len(bits):
            return (low + got.astype(F32))[0]
        low = low.astype(BF).astype(F32)
        half = half // 2
        high = (low[half:] + got[half:].astype(F32)).astype(BF)
        low = low[:half] + got[:half].astype(F32)


def all_reduce_tp(part):
    n = lax.axis_size("tp")
    rows = part.shape[0]
    sent = part.astype(BF).reshape((n, rows // n) + part.shape[1:])
    got = lax.all_to_all(sent, "tp", 0, 0)
    summed = jnp.sum(got.astype(F32), axis=0).astype(BF)
    return lax.all_gather(summed, "tp", axis=0, tiled=True)


def per_device(
    inputs,
    positions,
    cotangent,
    w_query,
    w_keyval,
    w_out,
    w_gate,
    w_up,
    w_down,
    gain_input,
    gain_query,
    gain_key,
    gain_attn,
    gain_prefn,
    gain_postfn,
):
    tokens = inputs[0]
    cot = cotangent[0]
    tok_pos = positions[0]
    n_ctx = lax.axis_size("ctx")
    n_tp = lax.axis_size("tp")
    count, width = tokens.shape
    qc = w_query.shape[1]
    kc = w_keyval.shape[1]
    heads = qc // HD
    index = natural_index()
    rows = w_query.shape[0]

    group = 128
    cols = qc + kc + w_out.shape[1]
    starts = (tok_pos[::group] // group).astype(BF)
    tail = jnp.zeros((16, cols), BF).at[0, : count // group].set(starts)
    first = jnp.concatenate([jnp.concatenate([w_query, w_keyval, w_out], axis=1), tail], axis=0)
    first_mine = gather_direct(first)
    first_all = with_other_core(first_mine)
    block_starts = jnp.stack([p[rows, : count // group] for p in first_mine]).astype(jnp.int32)
    pos_all = (block_starts.reshape(-1, 1) * group + jnp.arange(group, dtype=jnp.int32)[None]).reshape(-1)
    if rows % 16:
        first_all = [p[:rows] for p in first_all]
    first_all = in_order(first_all, index)
    normed_in, qkv, wqkv, wo = qkv_kernel(tokens, gain_input, index, first_all, qc + kc)

    gate_all = in_order(with_other_core(gather_doubling(w_gate)), index)
    up_all = in_order(with_other_core(gather_doubling(w_up)), index)
    down_all = in_order(with_other_core(gather_doubling(w_down)), index)

    cos_all, sin_all = rope_tables(pos_all)
    cosine, sine = cos_all[:count], sin_all[:count]
    q_raw = qkv[:, :qc].reshape(count, heads, HD)
    kv_part = qkv[:, qc:].astype(BF)

    kv_cols = jnp.concatenate(gather_direct(kv_part), axis=0)
    spread = jnp.broadcast_to(kv_cols[None], (n_tp,) + kv_cols.shape)
    kv_stack = lax.all_to_all(spread, "tp", 0, 0)
    kv_raw = jnp.concatenate([kv_stack[i] for i in range(n_tp)], axis=1)
    k_hat_all, k_factor_all = rms_parts(kv_raw[:, :HD].astype(F32))
    keys = rope(k_hat_all * gain_key, cos_all, sin_all).astype(BF)
    values = kv_raw[:, HD:]

    q_hat, q_factor = rms_parts(q_raw)
    queries = rope(q_hat * gain_query, cosine[:, None, :], sine[:, None, :]).astype(BF)
    visible = pos_all[None, :] <= tok_pos[:, None]

    scores, lses, outs = [], [], []
    for h in range(heads):
        s = dot_nt(queries[:, h], keys) * SCALE
        s = jnp.where(visible, s, -1e30)
        top = jnp.max(s, axis=-1, keepdims=True)
        w = jnp.exp(s - top)
        tot = jnp.sum(w, axis=-1, keepdims=True)
        outs.append((dot(w.astype(BF), values) / tot).astype(BF))
        lses.append(top + jnp.log(tot))
        scores.append(s)
    attn = jnp.concatenate(outs, axis=1)

    o_bf = all_reduce_tp(dot_nt(attn, wo))
    resid, normed_ff, mixed, p1, p2 = ff_forward(
        o_bf, tokens, gain_attn, gain_prefn, index, gate_all, up_all
    )
    f_bf = all_reduce_tp(ff_down(mixed, index, down_all, width))
    block_out, d_f, grad_postfn, d_gate, d_up, d_ff_part = ff_backward(
        f_bf, resid, cot, gain_postfn, p1, p2, index, gate_all, up_all, down_all
    )
    d_ff = all_reduce_tp(d_ff_part).astype(F32)
    ((down_keep, down_send),) = weight_grads(index, [(d_f, mixed)], "grad_down")
    grad_down = scatter_pair(down_keep, down_send)
    (gate_pair, up_pair) = weight_grads(index, [(normed_ff, d_gate), (normed_ff, d_up)], "grad_gate_up")
    grad_gate = scatter_pair(*gate_pair)
    grad_up = scatter_pair(*up_pair)

    o_hat, o_factor = rms_parts(o_bf.astype(F32))
    h_hat, h_factor = rms_parts(resid)
    upstream = cot.astype(F32)
    grad_prefn = jnp.sum(d_ff * h_hat, axis=0)
    d_resid = upstream + rms_back(d_ff, h_hat, h_factor, gain_prefn)
    grad_attn = jnp.sum(d_resid * o_hat, axis=0)
    d_o = rms_back(d_resid, o_hat, o_factor, gain_attn).astype(BF)
    ((out_keep, out_send),) = weight_grads(index, [(d_o, attn)], "grad_out")
    grad_out = scatter_pair(out_keep, out_send)
    d_attn = dot(d_o, wo).astype(BF)
    delta = jnp.sum(
        (d_attn.astype(F32) * attn.astype(F32)).reshape(count, heads, HD), axis=-1, keepdims=True
    )

    d_keys = jnp.zeros(keys.shape, F32)
    d_values = jnp.zeros(values.shape, F32)
    d_queries = []
    for h in range(heads):
        dah = d_attn[:, h * HD : (h + 1) * HD]
        probs = jnp.exp(scores[h] - lses[h])
        d_probs = dot_nt(dah, values)
        d_scores = (probs * (d_probs - delta[:, h])).astype(BF)
        d_queries.append(dot(d_scores, keys))
        d_keys = d_keys + dot_tn(d_scores, queries[:, h])
        d_values = d_values + dot_tn(probs.astype(BF), dah)

    quarter = count // n_tp
    dkv = jnp.concatenate([d_keys, d_values], axis=1).astype(BF)
    dkv = dkv.reshape(n_ctx, n_tp, quarter, 2 * HD).transpose(1, 0, 2, 3)
    dkv = lax.all_to_all(dkv, "tp", 0, 0)
    dkv = jnp.sum(dkv.astype(F32), axis=0).reshape(n_ctx * quarter, 2 * HD)
    dkv = scatter_ctx(dkv)
    at = lax.axis_index("tp") * quarter
    cos_q = lax.dynamic_slice_in_dim(cosine, at, quarter, 0)
    sin_q = lax.dynamic_slice_in_dim(sine, at, quarter, 0)
    khat_q = lax.dynamic_slice_in_dim(k_hat_all[:count], at, quarter, 0)
    kfac_q = lax.dynamic_slice_in_dim(k_factor_all[:count], at, quarter, 0)
    d_knorm = rope_back(dkv[:, :HD] * SCALE, cos_q, sin_q)
    grad_key_part = jnp.sum(d_knorm * khat_q, axis=0)
    d_kraw = rms_back(d_knorm, khat_q, kfac_q, gain_key)
    dkv_raw = jnp.concatenate([d_kraw, dkv[:, HD:]], axis=1).astype(BF)

    d_qnorm = rope_back(
        jnp.stack(d_queries, axis=1) * SCALE, cosine[:, None, :], sine[:, None, :]
    )
    grad_query_part = jnp.sum(d_qnorm * q_hat, axis=(0, 1))
    d_qraw = rms_back(d_qnorm, q_hat, q_factor, gain_query).astype(BF).reshape(count, qc)

    tail = jnp.concatenate([grad_query_part, grad_key_part])[None].astype(BF)
    tail = jnp.concatenate([tail, jnp.zeros((15, 2 * HD), BF)], axis=0)
    dkv_all = lax.all_gather(jnp.concatenate([dkv_raw, tail], axis=0), "tp", axis=0)
    dkv_full = dkv_all[:, :quarter].reshape(count, 2 * HD)
    gain_sums = jnp.sum(dkv_all[:, quarter].astype(F32), axis=0)
    dkv_cols = lax.dynamic_slice_in_dim(dkv_full, lax.axis_index("tp") * kc, kc, 1)
    d_qkv = jnp.concatenate([d_qraw, dkv_cols], axis=1)
    ((qkv_keep, qkv_send),) = weight_grads(index, [(normed_in, d_qkv)], "grad_qkv")
    grad_qkv = scatter_pair(qkv_keep, qkv_send)
    d_in = all_reduce_tp(dot_nt(d_qkv, wqkv)).astype(F32)
    x_hat, x_factor = rms_parts(tokens.astype(F32))
    grad_input = jnp.sum(d_in * x_hat, axis=0)
    input_grad = d_resid + rms_back(d_in, x_hat, x_factor, gain_input)

    blocks = 2 * n_ctx
    wide = jnp.stack([grad_input, grad_attn, grad_prefn, grad_postfn[0]])
    both = jnp.concatenate(
        [
            wide.reshape(4, blocks, -1).transpose(1, 0, 2).reshape(blocks, -1),
            gain_sums.reshape(2, blocks, -1).transpose(1, 0, 2).reshape(blocks, -1),
        ],
        axis=1,
    )
    both = jnp.take(both, index, axis=0)[:, None]
    mine = scatter_pair(both[:n_ctx], both[n_ctx:].astype(BF))[0]
    small = HD // blocks
    size = width // blocks
    base = 4 * size
    return (
        block_out[None],
        input_grad[None],
        grad_qkv[:, :qc],
        grad_qkv[:, qc:],
        grad_out,
        grad_gate,
        grad_up,
        grad_down,
        mine[:size],
        mine[base : base + small],
        mine[base + small :],
        mine[size : 2 * size],
        mine[2 * size : 3 * size],
        mine[3 * size : 4 * size],
    )


def solution(mesh):
    rows = P(("shard", "ctx"), "tp")
    tokens = P("shard", "ctx", None)
    gain = P(("shard", "ctx"))
    return jax.shard_map(
        per_device,
        mesh=mesh,
        in_specs=(tokens, P("shard", "ctx"), tokens) + (rows,) * 6 + (P(),) * 6,
        out_specs=(tokens, tokens) + (rows,) * 6 + (gain,) * 6,
        check_vma=False,
    )
```

```python
import jax
import jax.numpy as jnp
from jax import lax
from jax.experimental import pallas as pl
from jax.experimental.pallas import tpu as pltpu
from jax.sharding import PartitionSpec as P


HD = 256
EPS = 1e-06
THETA = 1000000.0
SCALE = 0.0625
GELU_C = 0.7978845608028654
BF = jnp.bfloat16
F32 = jnp.float32


def rms_parts(values):
    factor = lax.rsqrt(jnp.mean(values * values, axis=-1, keepdims=True) + EPS)
    return (values * factor, factor)


def rms_back(upstream, normed, factor, gain):
    scaled = upstream * gain
    inner = jnp.mean(scaled * normed, axis=-1, keepdims=True)
    return factor * (scaled - normed * inner)


def rotate_half(values):
    half = values.shape[-1] // 2
    return jnp.concatenate([-values[..., half:], values[..., :half]], axis=-1)


def rope_tables(tok_pos):
    half = HD // 2
    freq = THETA ** (-(jnp.arange(half, dtype=F32) * 2.0) / HD)
    angle = tok_pos.astype(F32)[:, None] * freq[None, :]
    cosine = jnp.cos(angle)
    sine = jnp.sin(angle)
    return (jnp.concatenate([cosine, cosine], axis=-1), jnp.concatenate([sine, sine], axis=-1))


def rope(values, cosine, sine):
    return values * cosine + rotate_half(values) * sine


def rope_back(values, cosine, sine):
    return values * cosine - rotate_half(values * sine)


def gelu_parts(gate):
    inner = GELU_C * (gate + 0.044715 * gate * gate * gate)
    tangent = jnp.tanh(inner)
    value = 0.5 * gate * (1.0 + tangent)
    slope = 0.5 * (1.0 + tangent) + 0.5 * gate * (1.0 - tangent * tangent) * GELU_C * (
        1.0 + 3.0 * 0.044715 * gate * gate
    )
    return (value, slope)


def dot(a, b):
    return jnp.dot(a, b, preferred_element_type=F32)


def dot_nt(a, b):
    return jnp.einsum("ik,jk->ij", a, b, preferred_element_type=F32)


def dot_tn(a, b):
    return jnp.einsum("ki,kj->ij", a, b, preferred_element_type=F32)


def xor_swap(x, axis, bit):
    size = lax.axis_size(axis)
    return lax.ppermute(x, axis, [(i, i ^ bit) for i in range(size)])


def after(x, *others):
    return lax.optimization_barrier((x,) + others)[0]


def bits_of(size):
    out = []
    bit = size >> 1
    while bit:
        out.append(bit)
        bit >>= 1
    return out


def xor_order(size):
    order = [0]
    for bit in bits_of(size):
        order = order + [k ^ bit for k in order]
    return order


def gather_doubling(x, hold=None):
    pieces, order = [x], [0]
    for bit in bits_of(lax.axis_size("ctx")):
        news = []
        for k, piece in zip(order, pieces, strict=True):
            if k and hold is not None:
                piece = after(piece, hold)
            news.append(xor_swap(piece, "ctx", bit))
        pieces, order = pieces + news, order + [k ^ bit for k in order]
    return pieces


def gather_direct(x):
    n = lax.axis_size("ctx")
    if n > 4:
        return gather_doubling(x)
    return [x] + [xor_swap(x, "ctx", k) for k in xor_order(n)[1:]]


def with_other_core(pieces):
    return pieces + [xor_swap(p, "shard", 1) for p in pieces]


def natural_index():
    n = lax.axis_size("ctx")
    me = lax.axis_index("ctx")
    shard = lax.axis_index("shard")
    order = jnp.array(xor_order(n), jnp.int32)
    mine = jnp.bitwise_xor(order, me)
    return jnp.concatenate([shard * n + mine, (1 - shard) * n + mine]).astype(jnp.int32)


def in_order(pieces, index):
    rows = pieces[0].shape[0]
    if rows % 16 == 0:
        return pieces
    whole = jnp.zeros((rows * len(pieces),) + pieces[0].shape[1:], pieces[0].dtype)
    for j, piece in enumerate(pieces):
        whole = lax.dynamic_update_slice_in_dim(whole, piece, index[j] * rows, 0)
    return [whole]


def load_pieces(index_ref, refs, target, sems, lanes=None):
    rows = target.shape[0] // len(refs)
    copies = []
    for j, ref in enumerate(refs):
        if len(refs) == 1:
            where = target
        else:
            start = pl.multiple_of(index_ref[j] * rows, 16)
            where = target.at[pl.ds(start, rows)]
        source = ref
        if ref.shape[0] != rows or lanes is not None:
            source = ref.at[pl.ds(0, rows), lanes if lanes is not None else slice(None)]
        copy = pltpu.make_async_copy(source, where, sems.at[j])
        copy.start()
        copies.append(copy)
    return copies


def vmem():
    return pl.BlockSpec(memory_space=pltpu.VMEM)


def smem():
    return pl.BlockSpec(memory_space=pltpu.SMEM)


def anywhere():
    return pl.BlockSpec(memory_space=pl.ANY)


def spans(total, step):
    return [(at, min(step, total - at)) for at in range(0, total, step)]


PARAMS = pltpu.CompilerParams(vmem_limit_bytes=56 * 1024 * 1024)


def qkv_kernel(tokens, gain, index, pieces, qkv_cols):
    rows, width = tokens.shape
    count = len(pieces)
    out_cols = pieces[0].shape[1] - qkv_cols

    def body(index_ref, x_ref, g_ref, *refs):
        ins = refs[:count]
        a_ref, qkv_ref, wq_ref, wo_ref, sem_a, sem_b = refs[count:]
        copies = load_pieces(index_ref, ins, wq_ref, sem_a, pl.ds(0, qkv_cols))
        copies += load_pieces(index_ref, ins, wo_ref, sem_b, pl.ds(qkv_cols, out_cols))
        x = x_ref[...].astype(F32)
        hat, _ = rms_parts(x)
        a = (hat * g_ref[...]).astype(BF)
        a_ref[...] = a
        for copy in copies:
            copy.wait()
        qkv_ref[...] = dot(a, wq_ref[...])

    return pl.pallas_call(
        body,
        out_shape=(
            jax.ShapeDtypeStruct((rows, width), BF),
            jax.ShapeDtypeStruct((rows, qkv_cols), F32),
            jax.ShapeDtypeStruct((width, qkv_cols), BF),
            jax.ShapeDtypeStruct((width, out_cols), BF),
        ),
        in_specs=[smem(), vmem(), vmem()] + [anywhere()] * count,
        out_specs=(vmem(),) * 4,
        scratch_shapes=[pltpu.SemaphoreType.DMA((count,))] * 2,
        compiler_params=PARAMS,
        name="qkv_kernel",
    )(index, tokens, gain[None], *pieces)


def ff_forward(o_proj, tokens, g_attn, g_pre, index, gate_pieces, up_pieces):
    rows, width = tokens.shape
    count = len(gate_pieces)
    ff = gate_pieces[0].shape[1]

    def body(index_ref, o_ref, x_ref, ga_ref, gp_ref, *refs):
        gates, ups = refs[:count], refs[count : 2 * count]
        h1_ref, b_ref, mix_ref, p1_ref, p2_ref, wg, wu, sem_g, sem_u = refs[2 * count :]
        copies = load_pieces(index_ref, gates, wg, sem_g)
        copies += load_pieces(index_ref, ups, wu, sem_u)
        o_hat, _ = rms_parts(o_ref[...].astype(F32))
        h1 = x_ref[...].astype(F32) + o_hat * ga_ref[...]
        h1_ref[...] = h1
        h_hat, _ = rms_parts(h1)
        b_ref[...] = (h_hat * gp_ref[...]).astype(BF)
        for copy in copies:
            copy.wait()

        def chunk(lanes):
            b = b_ref[...]
            gate = dot(b, wg[:, lanes])
            up = dot(b, wu[:, lanes])
            act, slope = gelu_parts(gate)
            mix_ref[:, lanes] = (act * up).astype(BF)
            p1_ref[:, lanes] = (up * slope).astype(BF)
            p2_ref[:, lanes] = act.astype(BF)

        whole = ff // 256

        @pl.loop(0, whole)
        def _(c):
            chunk(pl.ds(pl.multiple_of(c * 256, 256), 256))

        if ff % 256:
            chunk(pl.ds(whole * 256, ff % 256))

    wide = jax.ShapeDtypeStruct((rows, ff), BF)
    return pl.pallas_call(
        body,
        out_shape=(
            jax.ShapeDtypeStruct((rows, width), F32),
            jax.ShapeDtypeStruct((rows, width), BF),
            wide,
            wide,
            wide,
        ),
        in_specs=[smem()] + [vmem()] * 4 + [anywhere()] * (2 * count),
        out_specs=(vmem(),) * 5,
        scratch_shapes=[
            pltpu.VMEM((width, ff), BF),
            pltpu.VMEM((width, ff), BF),
            pltpu.SemaphoreType.DMA((count,)),
            pltpu.SemaphoreType.DMA((count,)),
        ],
        compiler_params=PARAMS,
        name="ff_forward",
    )(index, o_proj, tokens, g_attn[None], g_pre[None], *gate_pieces, *up_pieces)


def ff_down(mixed, index, pieces, width):
    rows, ff = mixed.shape
    count = len(pieces)

    def body(index_ref, mix_ref, *refs):
        ins = refs[:count]
        f_ref, wd, sems = refs[count:]
        for copy in load_pieces(index_ref, ins, wd, sems):
            copy.wait()
        for at, size in spans(width, 384):
            f_ref[:, at : at + size] = dot_nt(mix_ref[...], wd[at : at + size, :]).astype(BF)

    return pl.pallas_call(
        body,
        out_shape=jax.ShapeDtypeStruct((rows, width), BF),
        in_specs=[smem(), vmem()] + [anywhere()] * count,
        out_specs=vmem(),
        scratch_shapes=[pltpu.VMEM((width, ff), BF), pltpu.SemaphoreType.DMA((count,))],
        compiler_params=PARAMS,
        name="ff_down",
    )(index, mixed, *pieces)


def ff_backward(f_sum, h1, cot, g_post, p1, p2, index, gate_pieces, up_pieces, down_pieces):
    rows, width = h1.shape
    ff = p1.shape[1]
    count = len(gate_pieces)

    def body(index_ref, f_ref, h1_ref, cot_ref, gp_ref, p1_ref, p2_ref, *refs):
        gates, ups, downs = refs[:count], refs[count : 2 * count], refs[2 * count : 3 * count]
        (out_ref, df_ref, gpost_ref, dg_ref, du_ref, dff_ref, wg, wu, wd, sem_g, sem_u, sem_d) = refs[
            3 * count :
        ]
        copies_d = load_pieces(index_ref, downs, wd, sem_d)
        copies = load_pieces(index_ref, gates, wg, sem_g)
        copies += load_pieces(index_ref, ups, wu, sem_u)
        f_hat, factor = rms_parts(f_ref[...].astype(F32))
        gain = gp_ref[...]
        out_ref[...] = h1_ref[...] + f_hat * gain
        up_stream = cot_ref[...].astype(F32)
        gpost_ref[...] = jnp.sum(up_stream * f_hat, axis=0, keepdims=True)
        df_ref[...] = rms_back(up_stream, f_hat, factor, gain).astype(BF)
        for copy in copies_d:
            copy.wait()

        def chunk(lanes):
            d_mixed = dot(df_ref[...], wd[:, lanes])
            dg_ref[:, lanes] = (d_mixed * p1_ref[:, lanes].astype(F32)).astype(BF)
            du_ref[:, lanes] = (d_mixed * p2_ref[:, lanes].astype(F32)).astype(BF)

        whole = ff // 256

        @pl.loop(0, whole)
        def _(c):
            chunk(pl.ds(pl.multiple_of(c * 256, 256), 256))

        if ff % 256:
            chunk(pl.ds(whole * 256, ff % 256))
        for copy in copies:
            copy.wait()
        for at, size in spans(width, 384):
            dff_ref[:, at : at + size] = (
                dot_nt(dg_ref[...], wg[at : at + size, :]) + dot_nt(du_ref[...], wu[at : at + size, :])
            ).astype(BF)

    return pl.pallas_call(
        body,
        out_shape=(
            jax.ShapeDtypeStruct((rows, width), F32),
            jax.ShapeDtypeStruct((rows, width), BF),
            jax.ShapeDtypeStruct((1, width), F32),
            jax.ShapeDtypeStruct((rows, ff), BF),
            jax.ShapeDtypeStruct((rows, ff), BF),
            jax.ShapeDtypeStruct((rows, width), BF),
        ),
        in_specs=[smem()] + [vmem()] * 6 + [anywhere()] * (3 * count),
        out_specs=(vmem(),) * 6,
        scratch_shapes=[pltpu.VMEM((width, ff), BF)] * 3 + [pltpu.SemaphoreType.DMA((count,))] * 3,
        compiler_params=PARAMS,
        name="ff_backward",
    )(index, f_sum, h1, cot, g_post[None], p1, p2, *gate_pieces, *up_pieces, *down_pieces)


def weight_grads(index, groups):
    blocks = index.shape[0]
    half = blocks // 2
    rows, width = groups[0][0][0].shape
    size = width // blocks
    lefts, rights, plan = [], [], []
    for group in groups:
        at, places = 0, []
        for left, right in group:
            known = [i for i, seen in enumerate(lefts) if seen is left]
            if not known:
                lefts.append(left)
                known = [len(lefts) - 1]
            places.append((known[0], len(rights), at, right.shape[1]))
            rights.append(right)
            at += right.shape[1]
        plan.append((places, at))
    turned = [left.T.reshape(blocks, size, rows) for left in lefts]
    n_left, n_right, n_group = len(lefts), len(rights), len(groups)

    def body(index_ref, *refs):
        left_refs, right_refs = refs[:n_left], refs[n_left : n_left + n_right]
        outs = refs[n_left + n_right : n_left + n_right + 2 * n_group]
        held = refs[n_left + n_right + 2 * n_group : -n_group]
        sems = refs[-n_group:]

        for g, (places, _) in enumerate(plan):
            for side, first in ((1, half), (0, 0)):

                @pl.loop(0, half)
                def _(j, g=g, places=places, side=side, first=first):
                    for li, ri, at, cols in places:
                        held[g][first + j, :, at : at + cols] = dot(
                            left_refs[li][index_ref[first + j]], right_refs[ri][...]
                        ).astype(BF)
                    pltpu.make_async_copy(
                        held[g].at[first + j], outs[2 * g + side].at[j], sems[g].at[first + j]
                    ).start()

        for g in range(n_group):
            for side, first in ((1, half), (0, 0)):
                for j in range(half):
                    pltpu.make_async_copy(
                        held[g].at[first + j], outs[2 * g + side].at[j], sems[g].at[first + j]
                    ).wait()

    out_shape = []
    for _, cols in plan:
        out_shape += [jax.ShapeDtypeStruct((half, size, cols), BF)] * 2
    outs = pl.pallas_call(
        body,
        out_shape=out_shape,
        in_specs=[smem()] + [vmem()] * (n_left + n_right),
        out_specs=[anywhere()] * (2 * n_group),
        scratch_shapes=[pltpu.VMEM((blocks, size, cols), BF) for _, cols in plan]
        + [pltpu.SemaphoreType.DMA((blocks,))] * n_group,
        compiler_params=PARAMS,
    )(index, *turned, *rights)
    return [(outs[2 * g], outs[2 * g + 1]) for g in range(n_group)]


def scatter_ctx(x):
    bits = bits_of(lax.axis_size("ctx"))
    for place, bit in enumerate(reversed(bits)):
        half = x.shape[0] // 2
        got = xor_swap(x[half:].astype(BF), "ctx", bit)
        x = x[:half].astype(F32) + got.astype(F32)
        if place + 1 < len(bits):
            x = x.astype(BF)
    return x


def scatter_pair(keep, send):
    got = xor_swap(send, "shard", 1)
    bits = bits_of(lax.axis_size("ctx"))
    half = keep.shape[0] // 2
    low = keep[:half].astype(F32) + got[:half].astype(F32)
    high = (keep[half:].astype(F32) + got[half:].astype(F32)).astype(BF)
    for place, bit in enumerate(reversed(bits)):
        got = xor_swap(high, "ctx", bit)
        if place + 1 == len(bits):
            return (low + got.astype(F32))[0]
        low = low.astype(BF).astype(F32)
        half = half // 2
        high = (low[half:] + got[half:].astype(F32)).astype(BF)
        low = low[:half] + got[:half].astype(F32)


def all_reduce_tp(part):
    n = lax.axis_size("tp")
    rows = part.shape[0]
    sent = part.astype(BF).reshape((n, rows // n) + part.shape[1:])
    got = lax.all_to_all(sent, "tp", 0, 0)
    summed = jnp.sum(got.astype(F32), axis=0).astype(BF)
    return lax.all_gather(summed, "tp", axis=0, tiled=True)


def layer(
    inputs,
    positions,
    cotangent,
    w_query,
    w_keyval,
    w_out,
    w_gate,
    w_up,
    w_down,
    gain_input,
    gain_query,
    gain_key,
    gain_attn,
    gain_prefn,
    gain_postfn,
):
    tokens = inputs[0]
    cot = cotangent[0]
    tok_pos = positions[0]
    n_ctx = lax.axis_size("ctx")
    n_tp = lax.axis_size("tp")
    count, width = tokens.shape
    qc = w_query.shape[1]
    kc = w_keyval.shape[1]
    heads = qc // HD
    index = natural_index()
    rows = w_query.shape[0]

    group = 128
    cols = qc + kc + w_out.shape[1]
    starts = (tok_pos[::group] // group).astype(BF)
    tail = jnp.zeros((16, cols), BF).at[0, : count // group].set(starts)
    first = jnp.concatenate([jnp.concatenate([w_query, w_keyval, w_out], axis=1), tail], axis=0)
    first_mine = gather_direct(first)
    first_all = with_other_core(first_mine)
    block_starts = jnp.stack([p[rows, : count // group] for p in first_mine]).astype(jnp.int32)
    pos_all = (block_starts.reshape(-1, 1) * group + jnp.arange(group, dtype=jnp.int32)[None]).reshape(-1)
    if rows % 16:
        first_all = [p[:rows] for p in first_all]
    first_all = in_order(first_all, index)
    normed_in, qkv, wqkv, wo = qkv_kernel(tokens, gain_input, index, first_all, qc + kc)

    cos_all, sin_all = rope_tables(pos_all)
    cosine, sine = cos_all[:count], sin_all[:count]
    q_raw = qkv[:, :qc].reshape(count, heads, HD)
    kv_part = qkv[:, qc:].astype(BF)

    kv_cols = jnp.concatenate(gather_direct(kv_part), axis=0)
    spread = jnp.broadcast_to(kv_cols[None], (n_tp,) + kv_cols.shape)
    kv_stack = lax.all_to_all(spread, "tp", 0, 0)
    kv_raw = jnp.concatenate([kv_stack[i] for i in range(n_tp)], axis=1)
    k_hat_all, k_factor_all = rms_parts(kv_raw[:, :HD].astype(F32))
    keys = rope(k_hat_all * gain_key, cos_all, sin_all).astype(BF)
    values = kv_raw[:, HD:]

    q_hat, q_factor = rms_parts(q_raw)
    queries = rope(q_hat * gain_query, cosine[:, None, :], sine[:, None, :]).astype(BF)
    visible = pos_all[None, :] <= tok_pos[:, None]

    scores, lses, outs = [], [], []
    for h in range(heads):
        s = dot_nt(queries[:, h], keys) * SCALE
        s = jnp.where(visible, s, -1e30)
        top = jnp.max(s, axis=-1, keepdims=True)
        w = jnp.exp(s - top)
        tot = jnp.sum(w, axis=-1, keepdims=True)
        outs.append((dot(w.astype(BF), values) / tot).astype(BF))
        lses.append(top + jnp.log(tot))
        scores.append(s)
    attn = jnp.concatenate(outs, axis=1)

    o_part = dot_nt(attn, wo).astype(BF)
    gate_mine = gather_doubling(w_gate, kv_cols)
    up_mine = gather_doubling(w_up, kv_stack)
    o_bf = all_reduce_tp(o_part)
    down_mine = gather_doubling(w_down, o_bf)
    gate_all = in_order(with_other_core([after(p, o_bf) for p in gate_mine]), index)
    up_all = in_order(with_other_core([after(p, o_bf) for p in up_mine]), index)
    resid, normed_ff, mixed, p1, p2 = ff_forward(
        o_bf, tokens, gain_attn, gain_prefn, index, gate_all, up_all
    )
    down_all = in_order(with_other_core([after(p, o_bf) for p in down_mine]), index)
    f_bf = all_reduce_tp(ff_down(mixed, index, down_all, width))
    block_out, d_f, grad_postfn, d_gate, d_up, d_ff_part = ff_backward(
        f_bf, resid, cot, gain_postfn, p1, p2, index, gate_all, up_all, down_all
    )
    d_ff = all_reduce_tp(d_ff_part).astype(F32)
    (pair,) = weight_grads(index, [[(d_f, mixed)]])
    grad_down = scatter_pair(*pair)
    left = after(normed_ff, d_ff)
    pairs = weight_grads(index, [[(left, d_gate)], [(left, d_up)]])
    grad_gate = scatter_pair(*pairs[0])
    grad_up = scatter_pair(*pairs[1])

    o_hat, o_factor = rms_parts(o_bf.astype(F32))
    h_hat, h_factor = rms_parts(resid)
    upstream = cot.astype(F32)
    grad_prefn = jnp.sum(d_ff * h_hat, axis=0)
    d_resid = upstream + rms_back(d_ff, h_hat, h_factor, gain_prefn)
    grad_attn = jnp.sum(d_resid * o_hat, axis=0)
    d_o = rms_back(d_resid, o_hat, o_factor, gain_attn).astype(BF)
    d_attn = dot(d_o, wo).astype(BF)
    delta = jnp.sum(
        (d_attn.astype(F32) * attn.astype(F32)).reshape(count, heads, HD), axis=-1, keepdims=True
    )

    d_keys = jnp.zeros(keys.shape, F32)
    d_values = jnp.zeros(values.shape, F32)
    d_queries = []
    for h in range(heads):
        dah = d_attn[:, h * HD : (h + 1) * HD]
        probs = jnp.exp(scores[h] - lses[h])
        d_probs = dot_nt(dah, values)
        d_scores = (probs * (d_probs - delta[:, h])).astype(BF)
        d_queries.append(dot(d_scores, keys))
        d_keys = d_keys + dot_tn(d_scores, queries[:, h])
        d_values = d_values + dot_tn(probs.astype(BF), dah)

    quarter = count // n_tp
    dkv = jnp.concatenate([d_keys, d_values], axis=1).astype(BF)
    dkv = dkv.reshape(n_ctx, n_tp, quarter, 2 * HD).transpose(1, 0, 2, 3)
    dkv = lax.all_to_all(dkv, "tp", 0, 0)
    dkv = jnp.sum(dkv.astype(F32), axis=0).reshape(n_ctx * quarter, 2 * HD)
    dkv = scatter_ctx(dkv)
    at = lax.axis_index("tp") * quarter
    cos_q = lax.dynamic_slice_in_dim(cosine, at, quarter, 0)
    sin_q = lax.dynamic_slice_in_dim(sine, at, quarter, 0)
    khat_q = lax.dynamic_slice_in_dim(k_hat_all[:count], at, quarter, 0)
    kfac_q = lax.dynamic_slice_in_dim(k_factor_all[:count], at, quarter, 0)
    d_knorm = rope_back(dkv[:, :HD] * SCALE, cos_q, sin_q)
    grad_key_part = jnp.sum(d_knorm * khat_q, axis=0)
    d_kraw = rms_back(d_knorm, khat_q, kfac_q, gain_key)
    dkv_raw = jnp.concatenate([d_kraw, dkv[:, HD:]], axis=1).astype(BF)

    d_qnorm = rope_back(
        jnp.stack(d_queries, axis=1) * SCALE, cosine[:, None, :], sine[:, None, :]
    )
    grad_query_part = jnp.sum(d_qnorm * q_hat, axis=(0, 1))
    d_qraw = rms_back(d_qnorm, q_hat, q_factor, gain_query).astype(BF).reshape(count, qc)

    tail = jnp.concatenate([grad_query_part, grad_key_part])[None].astype(BF)
    tail = jnp.concatenate([tail, jnp.zeros((15, 2 * HD), BF)], axis=0)
    dkv_all = lax.all_gather(jnp.concatenate([dkv_raw, tail], axis=0), "tp", axis=0)
    dkv_full = dkv_all[:, :quarter].reshape(count, 2 * HD)
    gain_sums = jnp.sum(dkv_all[:, quarter].astype(F32), axis=0)
    dkv_cols = lax.dynamic_slice_in_dim(dkv_full, lax.axis_index("tp") * kc, kc, 1)
    d_qkv = jnp.concatenate([d_qraw, dkv_cols], axis=1)
    (pair,) = weight_grads(index, [[(normed_in, d_qkv), (d_o, attn)]])
    grad_heads = scatter_pair(*pair)
    d_in = all_reduce_tp(dot_nt(d_qkv, wqkv)).astype(F32)
    x_hat, x_factor = rms_parts(tokens.astype(F32))
    grad_input = jnp.sum(d_in * x_hat, axis=0)
    input_grad = d_resid + rms_back(d_in, x_hat, x_factor, gain_input)

    blocks = 2 * n_ctx
    wide = jnp.stack([grad_input, grad_attn, grad_prefn, grad_postfn[0]])
    both = jnp.concatenate(
        [
            wide.reshape(4, blocks, -1).transpose(1, 0, 2).reshape(blocks, -1),
            gain_sums.reshape(2, blocks, -1).transpose(1, 0, 2).reshape(blocks, -1),
        ],
        axis=1,
    )
    both = jnp.take(both, index, axis=0)[:, None]
    mine = scatter_pair(both[:n_ctx], both[n_ctx:].astype(BF))[0]
    small = HD // blocks
    size = width // blocks
    base = 4 * size
    return (
        block_out[None],
        input_grad[None],
        grad_heads[:, :qc],
        grad_heads[:, qc : qc + kc],
        grad_heads[:, qc + kc :],
        grad_gate,
        grad_up,
        grad_down,
        mine[:size],
        mine[base : base + small],
        mine[base + small :],
        mine[size : 2 * size],
        mine[2 * size : 3 * size],
        mine[3 * size : 4 * size],
    )


def solution(mesh):
    rows = P(("shard", "ctx"), "tp")
    tokens = P("shard", "ctx", None)
    gain = P(("shard", "ctx"))
    return jax.shard_map(
        layer,
        mesh=mesh,
        in_specs=(tokens, P("shard", "ctx"), tokens) + (rows,) * 6 + (P(),) * 6,
        out_specs=(tokens, tokens) + (rows,) * 6 + (gain,) * 6,
        check_vma=False,
    )
```

```python
import jax
import jax.numpy as jnp
from jax import lax
from jax.experimental import pallas as pl
from jax.experimental.pallas import tpu as pltpu
from jax.sharding import PartitionSpec as P


HD = 256
EPS = 1e-06
THETA = 1000000.0
SCALE = 0.0625
GELU_C = 0.7978845608028654
BF = jnp.bfloat16
F32 = jnp.float32


def rms_parts(values):
    factor = lax.rsqrt(jnp.mean(values * values, axis=-1, keepdims=True) + EPS)
    return (values * factor, factor)


def rms_back(upstream, normed, factor, gain):
    scaled = upstream * gain
    inner = jnp.mean(scaled * normed, axis=-1, keepdims=True)
    return factor * (scaled - normed * inner)


def rotate_half(values):
    half = values.shape[-1] // 2
    return jnp.concatenate([-values[..., half:], values[..., :half]], axis=-1)


def rope_tables(tok_pos):
    half = HD // 2
    freq = THETA ** (-(jnp.arange(half, dtype=F32) * 2.0) / HD)
    angle = tok_pos.astype(F32)[:, None] * freq[None, :]
    cosine = jnp.cos(angle)
    sine = jnp.sin(angle)
    return (jnp.concatenate([cosine, cosine], axis=-1), jnp.concatenate([sine, sine], axis=-1))


def rope(values, cosine, sine):
    return values * cosine + rotate_half(values) * sine


def rope_back(values, cosine, sine):
    return values * cosine - rotate_half(values * sine)


def gelu_parts(gate):
    inner = GELU_C * (gate + 0.044715 * gate * gate * gate)
    tangent = jnp.tanh(inner)
    value = 0.5 * gate * (1.0 + tangent)
    slope = 0.5 * (1.0 + tangent) + 0.5 * gate * (1.0 - tangent * tangent) * GELU_C * (
        1.0 + 3.0 * 0.044715 * gate * gate
    )
    return (value, slope)


def dot(a, b):
    return jnp.dot(a, b, preferred_element_type=F32)


def dot_nt(a, b):
    return jnp.einsum("ik,jk->ij", a, b, preferred_element_type=F32)


def dot_tn(a, b):
    return jnp.einsum("ki,kj->ij", a, b, preferred_element_type=F32)


def xor_swap(x, axis, bit):
    size = lax.axis_size(axis)
    return lax.ppermute(x, axis, [(i, i ^ bit) for i in range(size)])


def after(x, *others):
    return lax.optimization_barrier((x,) + others)[0]


def bits_of(size):
    out = []
    bit = size >> 1
    while bit:
        out.append(bit)
        bit >>= 1
    return out


def xor_order(size):
    order = [0]
    for bit in bits_of(size):
        order = order + [k ^ bit for k in order]
    return order


def gather_doubling(x, hold=None):
    pieces, order = [x], [0]
    for bit in bits_of(lax.axis_size("ctx")):
        news = []
        for k, piece in zip(order, pieces, strict=True):
            if k and hold is not None:
                piece = after(piece, hold)
            news.append(xor_swap(piece, "ctx", bit))
        pieces, order = pieces + news, order + [k ^ bit for k in order]
    return pieces


def gather_direct(x, hold=None):
    n = lax.axis_size("ctx")
    if n > 4:
        return gather_doubling(x, hold)
    return [x] + [xor_swap(x, "ctx", k) for k in xor_order(n)[1:]]


def with_other_core(pieces):
    return pieces + [xor_swap(p, "shard", 1) for p in pieces]


def natural_index():
    n = lax.axis_size("ctx")
    me = lax.axis_index("ctx")
    shard = lax.axis_index("shard")
    order = jnp.array(xor_order(n), jnp.int32)
    mine = jnp.bitwise_xor(order, me)
    return jnp.concatenate([shard * n + mine, (1 - shard) * n + mine]).astype(jnp.int32)


def in_order(pieces, index):
    rows = pieces[0].shape[0]
    if rows % 16 == 0:
        return pieces
    whole = jnp.zeros((rows * len(pieces),) + pieces[0].shape[1:], pieces[0].dtype)
    for j, piece in enumerate(pieces):
        whole = lax.dynamic_update_slice_in_dim(whole, piece, index[j] * rows, 0)
    return [whole]


def load_pieces(index_ref, refs, target, sems, lanes=None):
    rows = target.shape[0] // len(refs)
    copies = []
    for j, ref in enumerate(refs):
        if len(refs) == 1:
            where = target
        else:
            start = pl.multiple_of(index_ref[j] * rows, 16)
            where = target.at[pl.ds(start, rows)]
        source = ref
        if ref.shape[0] != rows or lanes is not None:
            source = ref.at[pl.ds(0, rows), lanes if lanes is not None else slice(None)]
        copy = pltpu.make_async_copy(source, where, sems.at[j])
        copy.start()
        copies.append(copy)
    return copies


def vmem():
    return pl.BlockSpec(memory_space=pltpu.VMEM)


def smem():
    return pl.BlockSpec(memory_space=pltpu.SMEM)


def anywhere():
    return pl.BlockSpec(memory_space=pl.ANY)


def spans(total, step):
    return [(at, min(step, total - at)) for at in range(0, total, step)]


PARAMS = pltpu.CompilerParams(vmem_limit_bytes=56 * 1024 * 1024)


def qkv_kernel(tokens, gain, index, pieces, qkv_cols):
    rows, width = tokens.shape
    count = len(pieces)
    out_cols = pieces[0].shape[1] - qkv_cols

    def body(index_ref, x_ref, g_ref, *refs):
        ins = refs[:count]
        a_ref, qkv_ref, wq_ref, wo_ref, sem_a, sem_b = refs[count:]
        copies = load_pieces(index_ref, ins, wq_ref, sem_a, pl.ds(0, qkv_cols))
        copies += load_pieces(index_ref, ins, wo_ref, sem_b, pl.ds(qkv_cols, out_cols))
        x = x_ref[...].astype(F32)
        hat, _ = rms_parts(x)
        a = (hat * g_ref[...]).astype(BF)
        a_ref[...] = a
        for copy in copies:
            copy.wait()
        qkv_ref[...] = dot(a, wq_ref[...])

    return pl.pallas_call(
        body,
        out_shape=(
            jax.ShapeDtypeStruct((rows, width), BF),
            jax.ShapeDtypeStruct((rows, qkv_cols), F32),
            jax.ShapeDtypeStruct((width, qkv_cols), BF),
            jax.ShapeDtypeStruct((width, out_cols), BF),
        ),
        in_specs=[smem(), vmem(), vmem()] + [anywhere()] * count,
        out_specs=(vmem(),) * 4,
        scratch_shapes=[pltpu.SemaphoreType.DMA((count,))] * 2,
        compiler_params=PARAMS,
        name="qkv_kernel",
    )(index, tokens, gain[None], *pieces)


def ff_forward(o_proj, tokens, g_attn, g_pre, index, gate_pieces, up_pieces):
    rows, width = tokens.shape
    count = len(gate_pieces)
    ff = gate_pieces[0].shape[1]

    def body(index_ref, o_ref, x_ref, ga_ref, gp_ref, *refs):
        gates, ups = refs[:count], refs[count : 2 * count]
        h1_ref, b_ref, mix_ref, p1_ref, p2_ref, wg, wu, sem_g, sem_u = refs[2 * count :]
        copies = load_pieces(index_ref, gates, wg, sem_g)
        copies += load_pieces(index_ref, ups, wu, sem_u)
        o_hat, _ = rms_parts(o_ref[...].astype(F32))
        h1 = x_ref[...].astype(F32) + o_hat * ga_ref[...]
        h1_ref[...] = h1
        h_hat, _ = rms_parts(h1)
        b_ref[...] = (h_hat * gp_ref[...]).astype(BF)
        for copy in copies:
            copy.wait()

        def chunk(lanes):
            b = b_ref[...]
            gate = dot(b, wg[:, lanes])
            up = dot(b, wu[:, lanes])
            act, slope = gelu_parts(gate)
            mix_ref[:, lanes] = (act * up).astype(BF)
            p1_ref[:, lanes] = (up * slope).astype(BF)
            p2_ref[:, lanes] = act.astype(BF)

        whole = ff // 256

        @pl.loop(0, whole)
        def _(c):
            chunk(pl.ds(pl.multiple_of(c * 256, 256), 256))

        if ff % 256:
            chunk(pl.ds(whole * 256, ff % 256))

    wide = jax.ShapeDtypeStruct((rows, ff), BF)
    return pl.pallas_call(
        body,
        out_shape=(
            jax.ShapeDtypeStruct((rows, width), F32),
            jax.ShapeDtypeStruct((rows, width), BF),
            wide,
            wide,
            wide,
        ),
        in_specs=[smem()] + [vmem()] * 4 + [anywhere()] * (2 * count),
        out_specs=(vmem(),) * 5,
        scratch_shapes=[
            pltpu.VMEM((width, ff), BF),
            pltpu.VMEM((width, ff), BF),
            pltpu.SemaphoreType.DMA((count,)),
            pltpu.SemaphoreType.DMA((count,)),
        ],
        compiler_params=PARAMS,
        name="ff_forward",
    )(index, o_proj, tokens, g_attn[None], g_pre[None], *gate_pieces, *up_pieces)


def ff_down(mixed, index, pieces, width):
    rows, ff = mixed.shape
    count = len(pieces)

    def body(index_ref, mix_ref, *refs):
        ins = refs[:count]
        f_ref, wd, sems = refs[count:]
        for copy in load_pieces(index_ref, ins, wd, sems):
            copy.wait()
        for at, size in spans(width, 384):
            f_ref[:, at : at + size] = dot_nt(mix_ref[...], wd[at : at + size, :]).astype(BF)

    return pl.pallas_call(
        body,
        out_shape=jax.ShapeDtypeStruct((rows, width), BF),
        in_specs=[smem(), vmem()] + [anywhere()] * count,
        out_specs=vmem(),
        scratch_shapes=[pltpu.VMEM((width, ff), BF), pltpu.SemaphoreType.DMA((count,))],
        compiler_params=PARAMS,
        name="ff_down",
    )(index, mixed, *pieces)


def ff_backward(f_sum, h1, cot, g_post, p1, p2, index, gate_pieces, up_pieces, down_pieces):
    rows, width = h1.shape
    ff = p1.shape[1]
    count = len(gate_pieces)

    def body(index_ref, f_ref, h1_ref, cot_ref, gp_ref, p1_ref, p2_ref, *refs):
        gates, ups, downs = refs[:count], refs[count : 2 * count], refs[2 * count : 3 * count]
        (out_ref, df_ref, gpost_ref, dg_ref, du_ref, dff_ref, wg, wu, wd, sem_g, sem_u, sem_d) = refs[
            3 * count :
        ]
        copies_d = load_pieces(index_ref, downs, wd, sem_d)
        copies = load_pieces(index_ref, gates, wg, sem_g)
        copies += load_pieces(index_ref, ups, wu, sem_u)
        f_hat, factor = rms_parts(f_ref[...].astype(F32))
        gain = gp_ref[...]
        out_ref[...] = h1_ref[...] + f_hat * gain
        up_stream = cot_ref[...].astype(F32)
        gpost_ref[...] = jnp.sum(up_stream * f_hat, axis=0, keepdims=True)
        df_ref[...] = rms_back(up_stream, f_hat, factor, gain).astype(BF)
        for copy in copies_d:
            copy.wait()

        def chunk(lanes):
            d_mixed = dot(df_ref[...], wd[:, lanes])
            dg_ref[:, lanes] = (d_mixed * p1_ref[:, lanes].astype(F32)).astype(BF)
            du_ref[:, lanes] = (d_mixed * p2_ref[:, lanes].astype(F32)).astype(BF)

        whole = ff // 256

        @pl.loop(0, whole)
        def _(c):
            chunk(pl.ds(pl.multiple_of(c * 256, 256), 256))

        if ff % 256:
            chunk(pl.ds(whole * 256, ff % 256))
        for copy in copies:
            copy.wait()
        for at, size in spans(width, 384):
            dff_ref[:, at : at + size] = (
                dot_nt(dg_ref[...], wg[at : at + size, :]) + dot_nt(du_ref[...], wu[at : at + size, :])
            ).astype(BF)

    return pl.pallas_call(
        body,
        out_shape=(
            jax.ShapeDtypeStruct((rows, width), F32),
            jax.ShapeDtypeStruct((rows, width), BF),
            jax.ShapeDtypeStruct((1, width), F32),
            jax.ShapeDtypeStruct((rows, ff), BF),
            jax.ShapeDtypeStruct((rows, ff), BF),
            jax.ShapeDtypeStruct((rows, width), BF),
        ),
        in_specs=[smem()] + [vmem()] * 6 + [anywhere()] * (3 * count),
        out_specs=(vmem(),) * 6,
        scratch_shapes=[pltpu.VMEM((width, ff), BF)] * 3 + [pltpu.SemaphoreType.DMA((count,))] * 3,
        compiler_params=PARAMS,
        name="ff_backward",
    )(index, f_sum, h1, cot, g_post[None], p1, p2, *gate_pieces, *up_pieces, *down_pieces)


def weight_grads(index, groups):
    blocks = index.shape[0]
    half = blocks // 2
    rows, width = groups[0][0][0].shape
    size = width // blocks
    lefts, rights, plan = [], [], []
    for group in groups:
        at, places = 0, []
        for left, right in group:
            known = [i for i, seen in enumerate(lefts) if seen is left]
            if not known:
                lefts.append(left)
                known = [len(lefts) - 1]
            places.append((known[0], len(rights), at, right.shape[1]))
            rights.append(right)
            at += right.shape[1]
        plan.append((places, at))
    tiled = size % 16 == 0
    turned = lefts if tiled else [left.T.reshape(blocks, size, rows) for left in lefts]
    n_left, n_right, n_group = len(lefts), len(rights), len(groups)

    def body(index_ref, *refs):
        left_refs, right_refs = refs[:n_left], refs[n_left : n_left + n_right]
        outs = refs[n_left + n_right : n_left + n_right + 2 * n_group]
        held = refs[n_left + n_right + 2 * n_group : -n_group]
        sems = refs[-n_group:]

        def copy(g, side, j):
            block = half * side + j
            if tiled:
                start = pl.multiple_of(index_ref[block] * size, 16)
                source = held[g].at[pl.ds(start, size)]
            else:
                source = held[g].at[block]
            return pltpu.make_async_copy(source, outs[2 * g + side].at[j], sems[g].at[block])

        for g, (places, _) in enumerate(plan):
            if tiled:
                for li, ri, at, cols in places:
                    for row, step in spans(width, 384):
                        held[g][row : row + step, at : at + cols] = dot_tn(
                            left_refs[li][:, row : row + step], right_refs[ri][...]
                        ).astype(BF)
            else:

                @pl.loop(0, blocks)
                def _(j, g=g, places=places):
                    for li, ri, at, cols in places:
                        held[g][j, :, at : at + cols] = dot(
                            left_refs[li][index_ref[j]], right_refs[ri][...]
                        ).astype(BF)

            for side in (1, 0):
                for j in range(half):
                    copy(g, side, j).start()
        for g in range(n_group):
            for side in (1, 0):
                for j in range(half):
                    copy(g, side, j).wait()

    out_shape = []
    for _, cols in plan:
        out_shape += [jax.ShapeDtypeStruct((half, size, cols), BF)] * 2
    outs = pl.pallas_call(
        body,
        out_shape=out_shape,
        in_specs=[smem()] + [vmem()] * (n_left + n_right),
        out_specs=[anywhere()] * (2 * n_group),
        scratch_shapes=[
            pltpu.VMEM((width, cols) if tiled else (blocks, size, cols), BF) for _, cols in plan
        ]
        + [pltpu.SemaphoreType.DMA((blocks,))] * n_group,
        compiler_params=PARAMS,
    )(index, *turned, *rights)
    return [(outs[2 * g], outs[2 * g + 1]) for g in range(n_group)]


def input_kernel(gathered, lead, quarter, wqkv, peers, peers_other, qc, d_resid, tokens, gain):
    rows, width = tokens.shape
    cols = wqkv.shape[1]
    kc = cols - qc
    n_tp = gathered.shape[0]
    order = xor_order(n_tp)
    count = len(peers)
    half = width // 2
    place = jnp.stack([lax.axis_index("shard"), lax.axis_index("tp")]).astype(jnp.int32)

    def body(place_ref, got_ref, own_ref, resid_ref, x_ref, gain_ref, *refs):
        mine, other = refs[:count], refs[count : 2 * count]
        out_ref, sum_ref, held, sem_a, sem_b = refs[2 * count :]
        shard, me = place_ref[0], place_ref[1]
        copies = []
        for refs_of, sems, side in ((mine, sem_a, shard), (other, sem_b, 1 - shard)):
            for i, ref in enumerate(refs_of):
                start = pl.multiple_of(side * half, 16)
                copy = pltpu.make_async_copy(ref, held.at[i, pl.ds(start, half)], sems.at[i])
                copy.start()
                copies.append(copy)

        def left(peer):
            lanes = pl.ds(pl.multiple_of(peer * kc, kc), kc)
            packed = got_ref[peer, :lead, :].reshape(rows // 2, 2 * qc)
            queries = jnp.concatenate([packed[:, :qc], packed[:, qc:]], axis=0)
            keys = jnp.concatenate(
                [got_ref[q, lead : lead + quarter, lanes] for q in range(n_tp)], axis=0
            )
            return jnp.concatenate([queries, keys], axis=1)

        total = dot_nt(left(me), own_ref[...])
        for copy in copies:
            copy.wait()
        for i in range(count):
            total = total + dot_nt(left(jnp.bitwise_xor(me, order[i + 1])), held[i])
        hat, factor = rms_parts(x_ref[...].astype(F32))
        sum_ref[...] = jnp.sum(total * hat, axis=0, keepdims=True)
        out_ref[...] = resid_ref[...] + rms_back(total, hat, factor, gain_ref[...])

    return pl.pallas_call(
        body,
        out_shape=(jax.ShapeDtypeStruct((rows, width), F32), jax.ShapeDtypeStruct((1, width), F32)),
        in_specs=[smem()] + [vmem()] * 5 + [anywhere()] * (2 * count),
        out_specs=(vmem(), vmem()),
        scratch_shapes=[
            pltpu.VMEM((count, width, cols), BF),
            pltpu.SemaphoreType.DMA((count,)),
            pltpu.SemaphoreType.DMA((count,)),
        ],
        compiler_params=PARAMS,
        name="input_kernel",
    )(place, gathered, wqkv, d_resid, tokens, gain[None], *peers, *peers_other)


def scatter_ctx(x):
    bits = bits_of(lax.axis_size("ctx"))
    for place, bit in enumerate(reversed(bits)):
        half = x.shape[0] // 2
        got = xor_swap(x[half:].astype(BF), "ctx", bit)
        x = x[:half].astype(F32) + got.astype(F32)
        if place + 1 < len(bits):
            x = x.astype(BF)
    return x


def scatter_pair(keep, send):
    parts = [keep, xor_swap(send, "shard", 1)]

    def total(first, last):
        return sum(part[first:last].astype(F32) for part in parts)

    end = keep.shape[0]
    for bit in reversed(bits_of(lax.axis_size("ctx"))):
        parts.append(xor_swap(total(end // 2, end).astype(BF), "ctx", bit))
        end = end // 2
    return total(0, 1)[0]


def all_reduce_tp(part):
    n = lax.axis_size("tp")
    rows = part.shape[0]
    sent = part.astype(BF).reshape((n, rows // n) + part.shape[1:])
    got = lax.all_to_all(sent, "tp", 0, 0)
    summed = jnp.sum(got.astype(F32), axis=0).astype(BF)
    return lax.all_gather(summed, "tp", axis=0, tiled=True)


def layer(
    inputs,
    positions,
    cotangent,
    w_query,
    w_keyval,
    w_out,
    w_gate,
    w_up,
    w_down,
    gain_input,
    gain_query,
    gain_key,
    gain_attn,
    gain_prefn,
    gain_postfn,
):
    tokens = inputs[0]
    cot = cotangent[0]
    tok_pos = positions[0]
    n_ctx = lax.axis_size("ctx")
    n_tp = lax.axis_size("tp")
    count, width = tokens.shape
    qc = w_query.shape[1]
    kc = w_keyval.shape[1]
    heads = qc // HD
    index = natural_index()
    rows = w_query.shape[0]

    group = 128
    cols = qc + kc + w_out.shape[1]
    starts = (tok_pos[::group] // group).astype(BF)
    tail = jnp.zeros((16, cols), BF).at[0, : count // group].set(starts)
    first = jnp.concatenate([jnp.concatenate([w_query, w_keyval, w_out], axis=1), tail], axis=0)
    first_mine = gather_direct(first)
    first_all = with_other_core(first_mine)
    block_starts = jnp.stack([p[rows, : count // group] for p in first_mine]).astype(jnp.int32)
    pos_all = (block_starts.reshape(-1, 1) * group + jnp.arange(group, dtype=jnp.int32)[None]).reshape(-1)
    if rows % 16:
        first_all = [p[:rows] for p in first_all]
    first_all = in_order(first_all, index)
    normed_in, qkv, wqkv, wo = qkv_kernel(tokens, gain_input, index, first_all, qc + kc)

    shard_rows = lax.dynamic_slice_in_dim(
        wqkv, lax.axis_index("shard") * (width // 2), width // 2, 0
    )
    tp_order = xor_order(n_tp)
    peers = [xor_swap(shard_rows, "tp", k) for k in tp_order[1:]]
    peers_other = [xor_swap(p, "shard", 1) for p in peers]

    cos_all, sin_all = rope_tables(pos_all)
    cosine, sine = cos_all[:count], sin_all[:count]
    q_raw = qkv[:, :qc].reshape(count, heads, HD)
    kv_part = qkv[:, qc:].astype(BF)

    kv_cols = jnp.concatenate(gather_direct(kv_part), axis=0)
    spread = jnp.broadcast_to(kv_cols[None], (n_tp,) + kv_cols.shape)
    kv_stack = lax.all_to_all(spread, "tp", 0, 0)
    kv_raw = jnp.concatenate([kv_stack[i] for i in range(n_tp)], axis=1)
    k_hat_all, k_factor_all = rms_parts(kv_raw[:, :HD].astype(F32))
    keys = rope(k_hat_all * gain_key, cos_all, sin_all).astype(BF)
    values = kv_raw[:, HD:]

    q_hat, q_factor = rms_parts(q_raw)
    queries = rope(q_hat * gain_query, cosine[:, None, :], sine[:, None, :]).astype(BF)
    visible = pos_all[None, :] <= tok_pos[:, None]

    scores, lses, outs = [], [], []
    for h in range(heads):
        s = dot_nt(queries[:, h], keys) * SCALE
        s = jnp.where(visible, s, -1e30)
        top = jnp.max(s, axis=-1, keepdims=True)
        w = jnp.exp(s - top)
        tot = jnp.sum(w, axis=-1, keepdims=True)
        outs.append((dot(w.astype(BF), values) / tot).astype(BF))
        lses.append(top + jnp.log(tot))
        scores.append(s)
    attn = jnp.concatenate(outs, axis=1)

    o_part = dot_nt(attn, wo).astype(BF)
    gate_mine = gather_doubling(w_gate, kv_cols)
    up_mine = gather_doubling(w_up, o_part)
    o_bf = all_reduce_tp(o_part)
    down_mine = gather_direct(w_down, o_bf)
    gate_all = in_order(with_other_core([after(p, o_bf) for p in gate_mine]), index)
    up_all = in_order(with_other_core([after(p, o_bf) for p in up_mine]), index)
    resid, normed_ff, mixed, p1, p2 = ff_forward(
        o_bf, tokens, gain_attn, gain_prefn, index, gate_all, up_all
    )
    down_all = in_order(with_other_core([after(p, o_bf) for p in down_mine]), index)
    f_bf = all_reduce_tp(ff_down(mixed, index, down_all, width))
    block_out, d_f, grad_postfn, d_gate, d_up, d_ff_part = ff_backward(
        f_bf, resid, cot, gain_postfn, p1, p2, index, gate_all, up_all, down_all
    )
    d_ff = all_reduce_tp(d_ff_part).astype(F32)
    (pair,) = weight_grads(index, [[(d_f, mixed)]])
    grad_down = scatter_pair(*pair)
    (pair,) = weight_grads(index, [[(normed_ff, d_gate)]])
    grad_gate = scatter_pair(*pair)
    (pair,) = weight_grads(index, [[(after(normed_ff, d_ff), d_up)]])
    grad_up = scatter_pair(*pair)

    o_hat, o_factor = rms_parts(o_bf.astype(F32))
    h_hat, h_factor = rms_parts(resid)
    upstream = cot.astype(F32)
    grad_prefn = jnp.sum(d_ff * h_hat, axis=0)
    d_resid = upstream + rms_back(d_ff, h_hat, h_factor, gain_prefn)
    grad_attn = jnp.sum(d_resid * o_hat, axis=0)
    d_o = rms_back(d_resid, o_hat, o_factor, gain_attn).astype(BF)
    d_attn = dot(d_o, wo).astype(BF)
    delta = jnp.sum(
        (d_attn.astype(F32) * attn.astype(F32)).reshape(count, heads, HD), axis=-1, keepdims=True
    )

    d_keys = jnp.zeros(keys.shape, F32)
    d_values = jnp.zeros(values.shape, F32)
    d_queries = []
    for h in range(heads):
        dah = d_attn[:, h * HD : (h + 1) * HD]
        probs = jnp.exp(scores[h] - lses[h])
        d_probs = dot_nt(dah, values)
        d_scores = (probs * (d_probs - delta[:, h])).astype(BF)
        d_queries.append(dot(d_scores, keys))
        d_keys = d_keys + dot_tn(d_scores, queries[:, h])
        d_values = d_values + dot_tn(probs.astype(BF), dah)

    quarter = count // n_tp
    dkv = jnp.concatenate([d_keys, d_values], axis=1).astype(BF)
    dkv = dkv.reshape(n_ctx, n_tp, quarter, 2 * HD).transpose(1, 0, 2, 3)
    dkv = lax.all_to_all(dkv, "tp", 0, 0)
    dkv = jnp.sum(dkv.astype(F32), axis=0).reshape(n_ctx * quarter, 2 * HD)
    dkv = scatter_ctx(dkv)
    at = lax.axis_index("tp") * quarter
    cos_q = lax.dynamic_slice_in_dim(cosine, at, quarter, 0)
    sin_q = lax.dynamic_slice_in_dim(sine, at, quarter, 0)
    khat_q = lax.dynamic_slice_in_dim(k_hat_all[:count], at, quarter, 0)
    kfac_q = lax.dynamic_slice_in_dim(k_factor_all[:count], at, quarter, 0)
    d_knorm = rope_back(dkv[:, :HD] * SCALE, cos_q, sin_q)
    grad_key_part = jnp.sum(d_knorm * khat_q, axis=0)
    d_kraw = rms_back(d_knorm, khat_q, kfac_q, gain_key)
    dkv_raw = jnp.concatenate([d_kraw, dkv[:, HD:]], axis=1).astype(BF)

    d_qnorm = rope_back(
        jnp.stack(d_queries, axis=1) * SCALE, cosine[:, None, :], sine[:, None, :]
    )
    grad_query_part = jnp.sum(d_qnorm * q_hat, axis=(0, 1))
    d_qraw = rms_back(d_qnorm, q_hat, q_factor, gain_query).astype(BF).reshape(count, qc)

    tail = jnp.concatenate([grad_query_part, grad_key_part])[None].astype(BF)
    tail = jnp.concatenate([tail, jnp.zeros((15, 2 * HD), BF)], axis=0)
    packed = jnp.concatenate([d_qraw[: count // 2], d_qraw[count // 2 :]], axis=1)
    packed = packed.reshape(-1, 2 * HD)
    lead = packed.shape[0]
    gathered = lax.all_gather(jnp.concatenate([packed, dkv_raw, tail], axis=0), "tp", axis=0)
    gain_sums = jnp.sum(gathered[:, lead + quarter].astype(F32), axis=0)
    at = lax.axis_index("tp") * kc
    dkv_cols = lax.dynamic_slice_in_dim(gathered[:, lead : lead + quarter], at, kc, 2).reshape(count, kc)
    d_qkv = jnp.concatenate([d_qraw, dkv_cols], axis=1)
    (pair,) = weight_grads(index, [[(normed_in, d_qkv), (d_o, attn)]])
    grad_heads = scatter_pair(*pair)
    input_grad, grad_input = input_kernel(
        gathered, lead, quarter, wqkv, peers, peers_other, qc, d_resid, tokens, gain_input
    )
    grad_input = grad_input[0]

    blocks = 2 * n_ctx
    wide = jnp.stack([grad_input, grad_attn, grad_prefn, grad_postfn[0]])
    both = jnp.concatenate(
        [
            wide.reshape(4, blocks, -1).transpose(1, 0, 2).reshape(blocks, -1),
            gain_sums.reshape(2, blocks, -1).transpose(1, 0, 2).reshape(blocks, -1),
        ],
        axis=1,
    )
    both = jnp.take(both, index, axis=0)[:, None]
    mine = scatter_pair(both[:n_ctx], both[n_ctx:].astype(BF))[0]
    small = HD // blocks
    size = width // blocks
    base = 4 * size
    return (
        block_out[None],
        input_grad[None],
        grad_heads[:, :qc],
        grad_heads[:, qc : qc + kc],
        grad_heads[:, qc + kc :],
        grad_gate,
        grad_up,
        grad_down,
        mine[:size],
        mine[base : base + small],
        mine[base + small :],
        mine[size : 2 * size],
        mine[2 * size : 3 * size],
        mine[3 * size : 4 * size],
    )


def solution(mesh):
    rows = P(("shard", "ctx"), "tp")
    tokens = P("shard", "ctx", None)
    gain = P(("shard", "ctx"))
    return jax.shard_map(
        layer,
        mesh=mesh,
        in_specs=(tokens, P("shard", "ctx"), tokens) + (rows,) * 6 + (P(),) * 6,
        out_specs=(tokens, tokens) + (rows,) * 6 + (gain,) * 6,
        check_vma=False,
    )
```

```python
import jax
import jax.numpy as jnp
from jax import lax
from jax.experimental import pallas as pl
from jax.experimental.pallas import tpu as pltpu
from jax.sharding import PartitionSpec as P


HD = 256
EPS = 1e-06
THETA = 1000000.0
SCALE = 0.0625
GELU_C = 0.7978845608028654
BF = jnp.bfloat16
F32 = jnp.float32


def rms_parts(values):
    factor = lax.rsqrt(jnp.mean(values * values, axis=-1, keepdims=True) + EPS)
    return (values * factor, factor)


def rms_back(upstream, normed, factor, gain):
    scaled = upstream * gain
    inner = jnp.mean(scaled * normed, axis=-1, keepdims=True)
    return factor * (scaled - normed * inner)


def rotate_half(values):
    half = values.shape[-1] // 2
    return jnp.concatenate([-values[..., half:], values[..., :half]], axis=-1)


def rope_tables(tok_pos):
    half = HD // 2
    freq = THETA ** (-(jnp.arange(half, dtype=F32) * 2.0) / HD)
    angle = tok_pos.astype(F32)[:, None] * freq[None, :]
    cosine = jnp.cos(angle)
    sine = jnp.sin(angle)
    return (jnp.concatenate([cosine, cosine], axis=-1), jnp.concatenate([sine, sine], axis=-1))


def rope(values, cosine, sine):
    return values * cosine + rotate_half(values) * sine


def rope_back(values, cosine, sine):
    return values * cosine - rotate_half(values * sine)


def gelu_parts(gate):
    inner = GELU_C * (gate + 0.044715 * gate * gate * gate)
    tangent = jnp.tanh(inner)
    value = 0.5 * gate * (1.0 + tangent)
    slope = 0.5 * (1.0 + tangent) + 0.5 * gate * (1.0 - tangent * tangent) * GELU_C * (
        1.0 + 3.0 * 0.044715 * gate * gate
    )
    return (value, slope)


def dot(a, b):
    return jnp.dot(a, b, preferred_element_type=F32)


def dot_nt(a, b):
    return jnp.einsum("ik,jk->ij", a, b, preferred_element_type=F32)


def dot_tn(a, b):
    return jnp.einsum("ki,kj->ij", a, b, preferred_element_type=F32)


def xor_swap(x, axis, bit):
    size = lax.axis_size(axis)
    return lax.ppermute(x, axis, [(i, i ^ bit) for i in range(size)])


def after(x, *others):
    return lax.optimization_barrier((x,) + others)[0]


def bits_of(size):
    out = []
    bit = size >> 1
    while bit:
        out.append(bit)
        bit >>= 1
    return out


def xor_order(size):
    order = [0]
    for bit in bits_of(size):
        order = order + [k ^ bit for k in order]
    return order


def gather_doubling(x, hold=None):
    pieces, order = [x], [0]
    for bit in bits_of(lax.axis_size("ctx")):
        news = []
        for k, piece in zip(order, pieces, strict=True):
            if k and hold is not None:
                piece = after(piece, hold)
            news.append(xor_swap(piece, "ctx", bit))
        pieces, order = pieces + news, order + [k ^ bit for k in order]
    return pieces


def gather_direct(x, hold=None):
    n = lax.axis_size("ctx")
    if n > 4:
        return gather_doubling(x, hold)
    return [x] + [xor_swap(x, "ctx", k) for k in xor_order(n)[1:]]


def with_other_core(pieces):
    return pieces + [xor_swap(p, "shard", 1) for p in pieces]


def natural_index():
    n = lax.axis_size("ctx")
    me = lax.axis_index("ctx")
    shard = lax.axis_index("shard")
    order = jnp.array(xor_order(n), jnp.int32)
    mine = jnp.bitwise_xor(order, me)
    return jnp.concatenate([shard * n + mine, (1 - shard) * n + mine]).astype(jnp.int32)


def in_order(pieces, index):
    rows = pieces[0].shape[0]
    if rows % 16 == 0:
        return pieces
    whole = jnp.zeros((rows * len(pieces),) + pieces[0].shape[1:], pieces[0].dtype)
    for j, piece in enumerate(pieces):
        whole = lax.dynamic_update_slice_in_dim(whole, piece, index[j] * rows, 0)
    return [whole]


def load_pieces(index_ref, refs, target, sems, lanes=None):
    rows = target.shape[0] // len(refs)
    copies = []
    for j, ref in enumerate(refs):
        if len(refs) == 1:
            where = target
        else:
            start = pl.multiple_of(index_ref[j] * rows, 16)
            where = target.at[pl.ds(start, rows)]
        source = ref
        if ref.shape[0] != rows or lanes is not None:
            source = ref.at[pl.ds(0, rows), lanes if lanes is not None else slice(None)]
        copy = pltpu.make_async_copy(source, where, sems.at[j])
        copy.start()
        copies.append(copy)
    return copies


def vmem():
    return pl.BlockSpec(memory_space=pltpu.VMEM)


def smem():
    return pl.BlockSpec(memory_space=pltpu.SMEM)


def anywhere():
    return pl.BlockSpec(memory_space=pl.ANY)


def spans(total, step):
    return [(at, min(step, total - at)) for at in range(0, total, step)]


PARAMS = pltpu.CompilerParams(vmem_limit_bytes=56 * 1024 * 1024)


def qkv_kernel(tokens, gain, index, pieces, qkv_cols):
    rows, width = tokens.shape
    count = len(pieces)
    out_cols = pieces[0].shape[1] - qkv_cols

    def body(index_ref, x_ref, g_ref, *refs):
        ins = refs[:count]
        a_ref, qkv_ref, wq_ref, wo_ref, sem_a, sem_b = refs[count:]
        copies = load_pieces(index_ref, ins, wq_ref, sem_a, pl.ds(0, qkv_cols))
        copies += load_pieces(index_ref, ins, wo_ref, sem_b, pl.ds(qkv_cols, out_cols))
        x = x_ref[...].astype(F32)
        hat, _ = rms_parts(x)
        a = (hat * g_ref[...]).astype(BF)
        a_ref[...] = a
        for copy in copies:
            copy.wait()
        qkv_ref[...] = dot(a, wq_ref[...])

    return pl.pallas_call(
        body,
        out_shape=(
            jax.ShapeDtypeStruct((rows, width), BF),
            jax.ShapeDtypeStruct((rows, qkv_cols), F32),
            jax.ShapeDtypeStruct((width, qkv_cols), BF),
            jax.ShapeDtypeStruct((width, out_cols), BF),
        ),
        in_specs=[smem(), vmem(), vmem()] + [anywhere()] * count,
        out_specs=(vmem(),) * 4,
        scratch_shapes=[pltpu.SemaphoreType.DMA((count,))] * 2,
        compiler_params=PARAMS,
        name="qkv_kernel",
    )(index, tokens, gain[None], *pieces)


def ff_forward(o_proj, tokens, g_attn, g_pre, index, gate_pieces, up_pieces):
    rows, width = tokens.shape
    count = len(gate_pieces)
    ff = gate_pieces[0].shape[1]

    def body(index_ref, o_ref, x_ref, ga_ref, gp_ref, *refs):
        gates, ups = refs[:count], refs[count : 2 * count]
        h1_ref, b_ref, mix_ref, p1_ref, p2_ref, wg, wu, sem_g, sem_u = refs[2 * count :]
        copies = load_pieces(index_ref, gates, wg, sem_g)
        copies += load_pieces(index_ref, ups, wu, sem_u)
        o_hat, _ = rms_parts(o_ref[...].astype(F32))
        h1 = x_ref[...].astype(F32) + o_hat * ga_ref[...]
        h1_ref[...] = h1
        h_hat, _ = rms_parts(h1)
        b_ref[...] = (h_hat * gp_ref[...]).astype(BF)
        for copy in copies:
            copy.wait()

        def chunk(lanes):
            b = b_ref[...]
            gate = dot(b, wg[:, lanes])
            up = dot(b, wu[:, lanes])
            act, slope = gelu_parts(gate)
            mix_ref[:, lanes] = (act * up).astype(BF)
            p1_ref[:, lanes] = (up * slope).astype(BF)
            p2_ref[:, lanes] = act.astype(BF)

        whole = ff // 256

        @pl.loop(0, whole)
        def _(c):
            chunk(pl.ds(pl.multiple_of(c * 256, 256), 256))

        if ff % 256:
            chunk(pl.ds(whole * 256, ff % 256))

    wide = jax.ShapeDtypeStruct((rows, ff), BF)
    return pl.pallas_call(
        body,
        out_shape=(
            jax.ShapeDtypeStruct((rows, width), F32),
            jax.ShapeDtypeStruct((rows, width), BF),
            wide,
            wide,
            wide,
        ),
        in_specs=[smem()] + [vmem()] * 4 + [anywhere()] * (2 * count),
        out_specs=(vmem(),) * 5,
        scratch_shapes=[
            pltpu.VMEM((width, ff), BF),
            pltpu.VMEM((width, ff), BF),
            pltpu.SemaphoreType.DMA((count,)),
            pltpu.SemaphoreType.DMA((count,)),
        ],
        compiler_params=PARAMS,
        name="ff_forward",
    )(index, o_proj, tokens, g_attn[None], g_pre[None], *gate_pieces, *up_pieces)


def ff_down(mixed, index, pieces, width):
    rows, ff = mixed.shape
    count = len(pieces)

    def body(index_ref, mix_ref, *refs):
        ins = refs[:count]
        f_ref, wd, sems = refs[count:]
        for copy in load_pieces(index_ref, ins, wd, sems):
            copy.wait()
        for at, size in spans(width, 384):
            f_ref[:, at : at + size] = dot_nt(mix_ref[...], wd[at : at + size, :]).astype(BF)

    return pl.pallas_call(
        body,
        out_shape=jax.ShapeDtypeStruct((rows, width), BF),
        in_specs=[smem(), vmem()] + [anywhere()] * count,
        out_specs=vmem(),
        scratch_shapes=[pltpu.VMEM((width, ff), BF), pltpu.SemaphoreType.DMA((count,))],
        compiler_params=PARAMS,
        name="ff_down",
    )(index, mixed, *pieces)


def ff_backward(f_sum, h1, cot, g_post, p1, p2, index, gate_pieces, up_pieces, down_pieces):
    rows, width = h1.shape
    ff = p1.shape[1]
    count = len(gate_pieces)

    def body(index_ref, f_ref, h1_ref, cot_ref, gp_ref, p1_ref, p2_ref, *refs):
        gates, ups, downs = refs[:count], refs[count : 2 * count], refs[2 * count : 3 * count]
        (out_ref, df_ref, gpost_ref, dg_ref, du_ref, dff_ref, wg, wu, wd, sem_g, sem_u, sem_d) = refs[
            3 * count :
        ]
        copies_d = load_pieces(index_ref, downs, wd, sem_d)
        copies = load_pieces(index_ref, gates, wg, sem_g)
        copies += load_pieces(index_ref, ups, wu, sem_u)
        f_hat, factor = rms_parts(f_ref[...].astype(F32))
        gain = gp_ref[...]
        out_ref[...] = h1_ref[...] + f_hat * gain
        up_stream = cot_ref[...].astype(F32)
        gpost_ref[...] = jnp.sum(up_stream * f_hat, axis=0, keepdims=True)
        df_ref[...] = rms_back(up_stream, f_hat, factor, gain).astype(BF)
        for copy in copies_d:
            copy.wait()

        def chunk(lanes):
            d_mixed = dot(df_ref[...], wd[:, lanes])
            dg_ref[:, lanes] = (d_mixed * p1_ref[:, lanes].astype(F32)).astype(BF)
            du_ref[:, lanes] = (d_mixed * p2_ref[:, lanes].astype(F32)).astype(BF)

        whole = ff // 256

        @pl.loop(0, whole)
        def _(c):
            chunk(pl.ds(pl.multiple_of(c * 256, 256), 256))

        if ff % 256:
            chunk(pl.ds(whole * 256, ff % 256))
        for copy in copies:
            copy.wait()
        for at, size in spans(width, 384):
            dff_ref[:, at : at + size] = (
                dot_nt(dg_ref[...], wg[at : at + size, :]) + dot_nt(du_ref[...], wu[at : at + size, :])
            ).astype(BF)

    return pl.pallas_call(
        body,
        out_shape=(
            jax.ShapeDtypeStruct((rows, width), F32),
            jax.ShapeDtypeStruct((rows, width), BF),
            jax.ShapeDtypeStruct((1, width), F32),
            jax.ShapeDtypeStruct((rows, ff), BF),
            jax.ShapeDtypeStruct((rows, ff), BF),
            jax.ShapeDtypeStruct((rows, width), BF),
        ),
        in_specs=[smem()] + [vmem()] * 6 + [anywhere()] * (3 * count),
        out_specs=(vmem(),) * 6,
        scratch_shapes=[pltpu.VMEM((width, ff), BF)] * 3 + [pltpu.SemaphoreType.DMA((count,))] * 3,
        compiler_params=PARAMS,
        name="ff_backward",
    )(index, f_sum, h1, cot, g_post[None], p1, p2, *gate_pieces, *up_pieces, *down_pieces)


def weight_grads(index, groups):
    blocks = index.shape[0]
    half = blocks // 2
    rows, width = groups[0][0][0].shape
    size = width // blocks
    lefts, rights, plan = [], [], []
    for group in groups:
        at, places = 0, []
        for left, right in group:
            known = [i for i, seen in enumerate(lefts) if seen is left]
            if not known:
                lefts.append(left)
                known = [len(lefts) - 1]
            places.append((known[0], len(rights), at, right.shape[1]))
            rights.append(right)
            at += right.shape[1]
        plan.append((places, at))
    tiled = size % 16 == 0
    turned = lefts if tiled else [left.T.reshape(blocks, size, rows) for left in lefts]
    n_left, n_right, n_group = len(lefts), len(rights), len(groups)

    def body(index_ref, *refs):
        left_refs, right_refs = refs[:n_left], refs[n_left : n_left + n_right]
        outs = refs[n_left + n_right : n_left + n_right + 2 * n_group]
        held = refs[n_left + n_right + 2 * n_group : -n_group]
        sems = refs[-n_group:]

        def copy(g, side, j):
            block = half * side + j
            if tiled:
                start = pl.multiple_of(index_ref[block] * size, 16)
                source = held[g].at[pl.ds(start, size)]
            else:
                source = held[g].at[block]
            return pltpu.make_async_copy(source, outs[2 * g + side].at[j], sems[g].at[block])

        for g, (places, _) in enumerate(plan):
            if tiled:
                for li, ri, at, cols in places:
                    for row, step in spans(width, 384):
                        held[g][row : row + step, at : at + cols] = dot_tn(
                            left_refs[li][:, row : row + step], right_refs[ri][...]
                        ).astype(BF)
            else:

                @pl.loop(0, blocks)
                def _(j, g=g, places=places):
                    for li, ri, at, cols in places:
                        held[g][j, :, at : at + cols] = dot(
                            left_refs[li][index_ref[j]], right_refs[ri][...]
                        ).astype(BF)

            for side in (1, 0):
                for j in range(half):
                    copy(g, side, j).start()
        for g in range(n_group):
            for side in (1, 0):
                for j in range(half):
                    copy(g, side, j).wait()

    out_shape = []
    for _, cols in plan:
        out_shape += [jax.ShapeDtypeStruct((half, size, cols), BF)] * 2
    outs = pl.pallas_call(
        body,
        out_shape=out_shape,
        in_specs=[smem()] + [vmem()] * (n_left + n_right),
        out_specs=[anywhere()] * (2 * n_group),
        scratch_shapes=[
            pltpu.VMEM((width, cols) if tiled else (blocks, size, cols), BF) for _, cols in plan
        ]
        + [pltpu.SemaphoreType.DMA((blocks,))] * n_group,
        compiler_params=PARAMS,
    )(index, *turned, *rights)
    return [(outs[2 * g], outs[2 * g + 1]) for g in range(n_group)]


def input_kernel(gathered, lead, quarter, wqkv, peers, peers_other, qc, d_resid, tokens, gain):
    rows, width = tokens.shape
    cols = wqkv.shape[1]
    kc = cols - qc
    n_tp = gathered.shape[0]
    order = xor_order(n_tp)
    count = len(peers)
    half = width // 2
    place = jnp.stack([lax.axis_index("shard"), lax.axis_index("tp")]).astype(jnp.int32)

    def body(place_ref, got_ref, own_ref, resid_ref, x_ref, gain_ref, *refs):
        mine, other = refs[:count], refs[count : 2 * count]
        out_ref, sum_ref, held, sem_a, sem_b = refs[2 * count :]
        shard, me = place_ref[0], place_ref[1]
        copies = []
        for refs_of, sems, side in ((mine, sem_a, shard), (other, sem_b, 1 - shard)):
            for i, ref in enumerate(refs_of):
                start = pl.multiple_of(side * half, 16)
                copy = pltpu.make_async_copy(ref, held.at[i, pl.ds(start, half)], sems.at[i])
                copy.start()
                copies.append(copy)

        def left(peer):
            lanes = pl.ds(pl.multiple_of(peer * kc, kc), kc)
            packed = got_ref[peer, :lead, :].reshape(rows // 2, 2 * qc)
            queries = jnp.concatenate([packed[:, :qc], packed[:, qc:]], axis=0)
            keys = jnp.concatenate(
                [got_ref[q, lead : lead + quarter, lanes] for q in range(n_tp)], axis=0
            )
            return jnp.concatenate([queries, keys], axis=1)

        total = dot_nt(left(me), own_ref[...])
        for copy in copies:
            copy.wait()
        for i in range(count):
            total = total + dot_nt(left(jnp.bitwise_xor(me, order[i + 1])), held[i])
        hat, factor = rms_parts(x_ref[...].astype(F32))
        sum_ref[...] = jnp.sum(total * hat, axis=0, keepdims=True)
        out_ref[...] = resid_ref[...] + rms_back(total, hat, factor, gain_ref[...])

    return pl.pallas_call(
        body,
        out_shape=(jax.ShapeDtypeStruct((rows, width), F32), jax.ShapeDtypeStruct((1, width), F32)),
        in_specs=[smem()] + [vmem()] * 5 + [anywhere()] * (2 * count),
        out_specs=(vmem(), vmem()),
        scratch_shapes=[
            pltpu.VMEM((count, width, cols), BF),
            pltpu.SemaphoreType.DMA((count,)),
            pltpu.SemaphoreType.DMA((count,)),
        ],
        compiler_params=PARAMS,
        name="input_kernel",
    )(place, gathered, wqkv, d_resid, tokens, gain[None], *peers, *peers_other)


def scatter_ctx(x):
    bits = bits_of(lax.axis_size("ctx"))
    for place, bit in enumerate(reversed(bits)):
        half = x.shape[0] // 2
        got = xor_swap(x[half:].astype(BF), "ctx", bit)
        x = x[:half].astype(F32) + got.astype(F32)
        if place + 1 < len(bits):
            x = x.astype(BF)
    return x


def scatter_pair(keep, send):
    parts = [keep, xor_swap(send, "shard", 1)]

    def total(first, last):
        return sum(part[first:last].astype(F32) for part in parts)

    end = keep.shape[0]
    for bit in reversed(bits_of(lax.axis_size("ctx"))):
        high = total(end // 2, end).astype(BF)
        parts.append(xor_swap(high, "ctx", bit))
        end = end // 2
    return total(0, 1)[0]


def scatter_split(keep, send):
    got = xor_swap(send, "shard", 1)
    sums = [[keep[i], got[i]] for i in range(keep.shape[0])]

    def total(parts):
        return sum(part.astype(F32) for part in parts)

    for bit in reversed(bits_of(lax.axis_size("ctx"))):
        half = len(sums) // 2
        for place in reversed(range(half, 2 * half)):
            block = total(sums[place]).astype(BF)
            sums[place - half].append(xor_swap(block, "ctx", bit))
        sums = sums[:half]
    return total(sums[0])


def all_reduce_tp(part):
    n = lax.axis_size("tp")
    rows = part.shape[0]
    sent = part.astype(BF).reshape((n, rows // n) + part.shape[1:])
    got = lax.all_to_all(sent, "tp", 0, 0)
    summed = jnp.sum(got.astype(F32), axis=0).astype(BF)
    return lax.all_gather(summed, "tp", axis=0, tiled=True)


def layer(
    inputs,
    positions,
    cotangent,
    w_query,
    w_keyval,
    w_out,
    w_gate,
    w_up,
    w_down,
    gain_input,
    gain_query,
    gain_key,
    gain_attn,
    gain_prefn,
    gain_postfn,
):
    tokens = inputs[0]
    cot = cotangent[0]
    tok_pos = positions[0]
    n_ctx = lax.axis_size("ctx")
    n_tp = lax.axis_size("tp")
    count, width = tokens.shape
    qc = w_query.shape[1]
    kc = w_keyval.shape[1]
    heads = qc // HD
    index = natural_index()
    rows = w_query.shape[0]

    group = 128
    cols = qc + kc + w_out.shape[1]
    starts = (tok_pos[::group] // group).astype(BF)
    tail = jnp.zeros((16, cols), BF).at[0, : count // group].set(starts)
    first = jnp.concatenate([jnp.concatenate([w_query, w_keyval, w_out], axis=1), tail], axis=0)
    first_mine = gather_direct(first)
    first_all = with_other_core(first_mine)
    block_starts = jnp.stack([p[rows, : count // group] for p in first_mine]).astype(jnp.int32)
    pos_all = (block_starts.reshape(-1, 1) * group + jnp.arange(group, dtype=jnp.int32)[None]).reshape(-1)
    if rows % 16:
        first_all = [p[:rows] for p in first_all]
    first_all = in_order(first_all, index)
    normed_in, qkv, wqkv, wo = qkv_kernel(tokens, gain_input, index, first_all, qc + kc)

    shard_rows = lax.dynamic_slice_in_dim(
        wqkv, lax.axis_index("shard") * (width // 2), width // 2, 0
    )
    tp_order = xor_order(n_tp)
    peers = [xor_swap(shard_rows, "tp", k) for k in tp_order[1:]]
    peers_other = [xor_swap(p, "shard", 1) for p in peers]

    cos_all, sin_all = rope_tables(pos_all)
    cosine, sine = cos_all[:count], sin_all[:count]
    q_raw = qkv[:, :qc].reshape(count, heads, HD)
    kv_part = qkv[:, qc:].astype(BF)

    kv_cols = jnp.concatenate(gather_direct(kv_part), axis=0)
    spread = jnp.broadcast_to(kv_cols[None], (n_tp,) + kv_cols.shape)
    kv_stack = lax.all_to_all(spread, "tp", 0, 0)
    kv_raw = jnp.concatenate([kv_stack[i] for i in range(n_tp)], axis=1)
    k_hat_all, k_factor_all = rms_parts(kv_raw[:, :HD].astype(F32))
    keys = rope(k_hat_all * gain_key, cos_all, sin_all).astype(BF)
    values = kv_raw[:, HD:]

    q_hat, q_factor = rms_parts(q_raw)
    queries = rope(q_hat * gain_query, cosine[:, None, :], sine[:, None, :]).astype(BF)
    visible = pos_all[None, :] <= tok_pos[:, None]

    scores, lses, outs = [], [], []
    for h in range(heads):
        s = dot_nt(queries[:, h], keys) * SCALE
        s = jnp.where(visible, s, -1e30)
        top = jnp.max(s, axis=-1, keepdims=True)
        w = jnp.exp(s - top)
        tot = jnp.sum(w, axis=-1, keepdims=True)
        outs.append((dot(w.astype(BF), values) / tot).astype(BF))
        lses.append(top + jnp.log(tot))
        scores.append(s)
    attn = jnp.concatenate(outs, axis=1)

    o_part = dot_nt(attn, wo).astype(BF)
    gate_mine = gather_doubling(w_gate, kv_cols)
    up_mine = gather_doubling(w_up, o_part)
    o_bf = all_reduce_tp(o_part)
    down_mine = gather_direct(w_down, o_bf)
    gate_all = in_order(with_other_core([after(p, o_part) for p in gate_mine]), index)
    up_all = in_order(with_other_core([after(p, o_part) for p in up_mine[:-1]] + [after(up_mine[-1], o_bf)]), index)
    resid, normed_ff, mixed, p1, p2 = ff_forward(
        o_bf, tokens, gain_attn, gain_prefn, index, gate_all, up_all
    )
    down_all = in_order(with_other_core([after(p, o_bf) for p in down_mine]), index)
    f_bf = all_reduce_tp(ff_down(mixed, index, down_all, width))
    block_out, d_f, grad_postfn, d_gate, d_up, d_ff_part = ff_backward(
        f_bf, resid, cot, gain_postfn, p1, p2, index, gate_all, up_all, down_all
    )
    d_ff = all_reduce_tp(d_ff_part).astype(F32)
    (pair,) = weight_grads(index, [[(d_f, mixed)]])
    grad_down = scatter_split(*pair)
    (pair,) = weight_grads(index, [[(normed_ff, d_gate)]])
    grad_gate = scatter_split(*pair)
    (pair,) = weight_grads(index, [[(after(normed_ff, d_ff), d_up)]])
    grad_up = scatter_split(*pair)

    o_hat, o_factor = rms_parts(o_bf.astype(F32))
    h_hat, h_factor = rms_parts(resid)
    upstream = cot.astype(F32)
    grad_prefn = jnp.sum(d_ff * h_hat, axis=0)
    d_resid = upstream + rms_back(d_ff, h_hat, h_factor, gain_prefn)
    grad_attn = jnp.sum(d_resid * o_hat, axis=0)
    d_o = rms_back(d_resid, o_hat, o_factor, gain_attn).astype(BF)
    d_attn = dot(d_o, wo).astype(BF)
    delta = jnp.sum(
        (d_attn.astype(F32) * attn.astype(F32)).reshape(count, heads, HD), axis=-1, keepdims=True
    )

    d_keys = jnp.zeros(keys.shape, F32)
    d_values = jnp.zeros(values.shape, F32)
    d_queries = []
    for h in range(heads):
        dah = d_attn[:, h * HD : (h + 1) * HD]
        probs = jnp.exp(scores[h] - lses[h])
        d_probs = dot_nt(dah, values)
        d_scores = (probs * (d_probs - delta[:, h])).astype(BF)
        d_queries.append(dot(d_scores, keys))
        d_keys = d_keys + dot_tn(d_scores, queries[:, h])
        d_values = d_values + dot_tn(probs.astype(BF), dah)

    quarter = count // n_tp
    dkv = jnp.concatenate([d_keys, d_values], axis=1).astype(BF)
    dkv = dkv.reshape(n_ctx, n_tp, quarter, 2 * HD).transpose(1, 0, 2, 3)
    dkv = lax.all_to_all(dkv, "tp", 0, 0)
    dkv = jnp.sum(dkv.astype(F32), axis=0).reshape(n_ctx * quarter, 2 * HD)
    dkv = scatter_ctx(dkv)
    at = lax.axis_index("tp") * quarter
    cos_q = lax.dynamic_slice_in_dim(cosine, at, quarter, 0)
    sin_q = lax.dynamic_slice_in_dim(sine, at, quarter, 0)
    khat_q = lax.dynamic_slice_in_dim(k_hat_all[:count], at, quarter, 0)
    kfac_q = lax.dynamic_slice_in_dim(k_factor_all[:count], at, quarter, 0)
    d_knorm = rope_back(dkv[:, :HD] * SCALE, cos_q, sin_q)
    grad_key_part = jnp.sum(d_knorm * khat_q, axis=0)
    d_kraw = rms_back(d_knorm, khat_q, kfac_q, gain_key)
    dkv_raw = jnp.concatenate([d_kraw, dkv[:, HD:]], axis=1).astype(BF)

    d_qnorm = rope_back(
        jnp.stack(d_queries, axis=1) * SCALE, cosine[:, None, :], sine[:, None, :]
    )
    grad_query_part = jnp.sum(d_qnorm * q_hat, axis=(0, 1))
    d_qraw = rms_back(d_qnorm, q_hat, q_factor, gain_query).astype(BF).reshape(count, qc)

    tail = jnp.concatenate([grad_query_part, grad_key_part])[None].astype(BF)
    tail = jnp.concatenate([tail, jnp.zeros((15, 2 * HD), BF)], axis=0)
    packed = jnp.concatenate([d_qraw[: count // 2], d_qraw[count // 2 :]], axis=1)
    packed = packed.reshape(-1, 2 * HD)
    lead = packed.shape[0]
    gathered = lax.all_gather(jnp.concatenate([packed, dkv_raw, tail], axis=0), "tp", axis=0)
    gain_sums = jnp.sum(gathered[:, lead + quarter].astype(F32), axis=0)
    at = lax.axis_index("tp") * kc
    dkv_cols = lax.dynamic_slice_in_dim(gathered[:, lead : lead + quarter], at, kc, 2).reshape(count, kc)
    d_qkv = jnp.concatenate([d_qraw, dkv_cols], axis=1)
    (pair,) = weight_grads(index, [[(normed_in, d_qkv), (d_o, attn)]])
    grad_heads = scatter_pair(*pair)
    input_grad, grad_input = input_kernel(
        gathered, lead, quarter, wqkv, peers, peers_other, qc, d_resid, tokens, gain_input
    )
    grad_input = grad_input[0]

    blocks = 2 * n_ctx
    wide = jnp.stack([grad_input, grad_attn, grad_prefn, grad_postfn[0]])
    both = jnp.concatenate(
        [
            wide.reshape(4, blocks, -1).transpose(1, 0, 2).reshape(blocks, -1),
            gain_sums.reshape(2, blocks, -1).transpose(1, 0, 2).reshape(blocks, -1),
        ],
        axis=1,
    )
    both = jnp.take(both, index, axis=0)[:, None]
    mine = scatter_pair(both[:n_ctx], both[n_ctx:].astype(BF))[0]
    small = HD // blocks
    size = width // blocks
    base = 4 * size
    return (
        block_out[None],
        input_grad[None],
        grad_heads[:, :qc],
        grad_heads[:, qc : qc + kc],
        grad_heads[:, qc + kc :],
        grad_gate,
        grad_up,
        grad_down,
        mine[:size],
        mine[base : base + small],
        mine[base + small :],
        mine[size : 2 * size],
        mine[2 * size : 3 * size],
        mine[3 * size : 4 * size],
    )


def solution(mesh):
    rows = P(("shard", "ctx"), "tp")
    tokens = P("shard", "ctx", None)
    gain = P(("shard", "ctx"))
    return jax.shard_map(
        layer,
        mesh=mesh,
        in_specs=(tokens, P("shard", "ctx"), tokens) + (rows,) * 6 + (P(),) * 6,
        out_specs=(tokens, tokens) + (rows,) * 6 + (gain,) * 6,
        check_vma=False,
    )
```

```python
import jax
import jax.numpy as jnp
from jax import lax
from jax.experimental import pallas as pl
from jax.experimental.pallas import tpu as pltpu
from jax.sharding import PartitionSpec as P


HD = 256
EPS = 1e-06
THETA = 1000000.0
SCALE = 0.0625
GELU_C = 0.7978845608028654
BF = jnp.bfloat16
F32 = jnp.float32


def rms_parts(values):
    factor = lax.rsqrt(jnp.mean(values * values, axis=-1, keepdims=True) + EPS)
    return (values * factor, factor)


def rms_back(upstream, normed, factor, gain):
    scaled = upstream * gain
    inner = jnp.mean(scaled * normed, axis=-1, keepdims=True)
    return factor * (scaled - normed * inner)


def rotate_half(values):
    half = values.shape[-1] // 2
    return jnp.concatenate([-values[..., half:], values[..., :half]], axis=-1)


def rope_tables(tok_pos):
    half = HD // 2
    freq = THETA ** (-(jnp.arange(half, dtype=F32) * 2.0) / HD)
    angle = tok_pos.astype(F32)[:, None] * freq[None, :]
    cosine = jnp.cos(angle)
    sine = jnp.sin(angle)
    return (jnp.concatenate([cosine, cosine], axis=-1), jnp.concatenate([sine, sine], axis=-1))


def rope(values, cosine, sine):
    return values * cosine + rotate_half(values) * sine


def rope_back(values, cosine, sine):
    return values * cosine - rotate_half(values * sine)


def gelu_parts(gate):
    inner = GELU_C * (gate + 0.044715 * gate * gate * gate)
    tangent = jnp.tanh(inner)
    value = 0.5 * gate * (1.0 + tangent)
    slope = 0.5 * (1.0 + tangent) + 0.5 * gate * (1.0 - tangent * tangent) * GELU_C * (
        1.0 + 3.0 * 0.044715 * gate * gate
    )
    return (value, slope)


def dot(a, b):
    return jnp.dot(a, b, preferred_element_type=F32)


def dot_nt(a, b):
    return jnp.einsum("ik,jk->ij", a, b, preferred_element_type=F32)


def dot_tn(a, b):
    return jnp.einsum("ki,kj->ij", a, b, preferred_element_type=F32)


def xor_swap(x, axis, bit):
    size = lax.axis_size(axis)
    return lax.ppermute(x, axis, [(i, i ^ bit) for i in range(size)])


def after(x, *others):
    return lax.optimization_barrier((x,) + others)[0]


def bits_of(size):
    out = []
    bit = size >> 1
    while bit:
        out.append(bit)
        bit >>= 1
    return out


def xor_order(size):
    order = [0]
    for bit in bits_of(size):
        order = order + [k ^ bit for k in order]
    return order


def gather_doubling(x, hold=None):
    pieces, order = [x], [0]
    for bit in bits_of(lax.axis_size("ctx")):
        news = []
        for k, piece in zip(order, pieces, strict=True):
            if k and hold is not None:
                piece = after(piece, hold)
            news.append(xor_swap(piece, "ctx", bit))
        pieces, order = pieces + news, order + [k ^ bit for k in order]
    return pieces


def gather_direct(x, hold=None):
    n = lax.axis_size("ctx")
    if n > 4:
        return gather_doubling(x, hold)
    return [x] + [xor_swap(x, "ctx", k) for k in xor_order(n)[1:]]


def with_other_core(pieces):
    return pieces + [xor_swap(p, "shard", 1) for p in pieces]


def natural_index():
    n = lax.axis_size("ctx")
    me = lax.axis_index("ctx")
    shard = lax.axis_index("shard")
    order = jnp.array(xor_order(n), jnp.int32)
    mine = jnp.bitwise_xor(order, me)
    return jnp.concatenate([shard * n + mine, (1 - shard) * n + mine]).astype(jnp.int32)


def in_order(pieces, index):
    rows = pieces[0].shape[0]
    if rows % 16 == 0:
        return pieces
    whole = jnp.zeros((rows * len(pieces),) + pieces[0].shape[1:], pieces[0].dtype)
    for j, piece in enumerate(pieces):
        whole = lax.dynamic_update_slice_in_dim(whole, piece, index[j] * rows, 0)
    return [whole]


def load_pieces(index_ref, refs, target, sems, lanes=None):
    rows = target.shape[0] // len(refs)
    copies = []
    for j, ref in enumerate(refs):
        if len(refs) == 1:
            where = target
        else:
            start = pl.multiple_of(index_ref[j] * rows, 16)
            where = target.at[pl.ds(start, rows)]
        source = ref
        if ref.shape[0] != rows or lanes is not None:
            source = ref.at[pl.ds(0, rows), lanes if lanes is not None else slice(None)]
        copy = pltpu.make_async_copy(source, where, sems.at[j])
        copy.start()
        copies.append(copy)
    return copies


def vmem():
    return pl.BlockSpec(memory_space=pltpu.VMEM)


def smem():
    return pl.BlockSpec(memory_space=pltpu.SMEM)


def anywhere():
    return pl.BlockSpec(memory_space=pl.ANY)


def spans(total, step):
    return [(at, min(step, total - at)) for at in range(0, total, step)]


PARAMS = pltpu.CompilerParams(vmem_limit_bytes=56 * 1024 * 1024)


def qkv_kernel(tokens, gain, index, pieces, qkv_cols):
    rows, width = tokens.shape
    count = len(pieces)
    out_cols = pieces[0].shape[1] - qkv_cols

    def body(index_ref, x_ref, g_ref, *refs):
        ins = refs[:count]
        a_ref, qkv_ref, wq_ref, wo_ref, sem_a, sem_b = refs[count:]
        copies = load_pieces(index_ref, ins, wq_ref, sem_a, pl.ds(0, qkv_cols))
        copies += load_pieces(index_ref, ins, wo_ref, sem_b, pl.ds(qkv_cols, out_cols))
        x = x_ref[...].astype(F32)
        hat, _ = rms_parts(x)
        a = (hat * g_ref[...]).astype(BF)
        a_ref[...] = a
        for copy in copies:
            copy.wait()
        qkv_ref[...] = dot(a, wq_ref[...])

    return pl.pallas_call(
        body,
        out_shape=(
            jax.ShapeDtypeStruct((rows, width), BF),
            jax.ShapeDtypeStruct((rows, qkv_cols), F32),
            jax.ShapeDtypeStruct((width, qkv_cols), BF),
            jax.ShapeDtypeStruct((width, out_cols), BF),
        ),
        in_specs=[smem(), vmem(), vmem()] + [anywhere()] * count,
        out_specs=(vmem(),) * 4,
        scratch_shapes=[pltpu.SemaphoreType.DMA((count,))] * 2,
        compiler_params=PARAMS,
        name="qkv_kernel",
    )(index, tokens, gain[None], *pieces)


def ff_forward(o_proj, tokens, g_attn, g_pre, index, gate_pieces, up_pieces):
    rows, width = tokens.shape
    count = len(gate_pieces)
    ff = gate_pieces[0].shape[1]

    def body(index_ref, o_ref, x_ref, ga_ref, gp_ref, *refs):
        gates, ups = refs[:count], refs[count : 2 * count]
        h1_ref, b_ref, mix_ref, p1_ref, p2_ref, wg, wu, sem_g, sem_u = refs[2 * count :]
        copies = load_pieces(index_ref, gates, wg, sem_g)
        copies += load_pieces(index_ref, ups, wu, sem_u)
        o_hat, _ = rms_parts(o_ref[...].astype(F32))
        h1 = x_ref[...].astype(F32) + o_hat * ga_ref[...]
        h1_ref[...] = h1
        h_hat, _ = rms_parts(h1)
        b_ref[...] = (h_hat * gp_ref[...]).astype(BF)
        for copy in copies:
            copy.wait()

        def chunk(lanes):
            b = b_ref[...]
            gate = dot(b, wg[:, lanes])
            up = dot(b, wu[:, lanes])
            act, slope = gelu_parts(gate)
            mix_ref[:, lanes] = (act * up).astype(BF)
            p1_ref[:, lanes] = (up * slope).astype(BF)
            p2_ref[:, lanes] = act.astype(BF)

        whole = ff // 256

        @pl.loop(0, whole)
        def _(c):
            chunk(pl.ds(pl.multiple_of(c * 256, 256), 256))

        if ff % 256:
            chunk(pl.ds(whole * 256, ff % 256))

    wide = jax.ShapeDtypeStruct((rows, ff), BF)
    return pl.pallas_call(
        body,
        out_shape=(
            jax.ShapeDtypeStruct((rows, width), F32),
            jax.ShapeDtypeStruct((rows, width), BF),
            wide,
            wide,
            wide,
        ),
        in_specs=[smem()] + [vmem()] * 4 + [anywhere()] * (2 * count),
        out_specs=(vmem(),) * 5,
        scratch_shapes=[
            pltpu.VMEM((width, ff), BF),
            pltpu.VMEM((width, ff), BF),
            pltpu.SemaphoreType.DMA((count,)),
            pltpu.SemaphoreType.DMA((count,)),
        ],
        compiler_params=PARAMS,
        name="ff_forward",
    )(index, o_proj, tokens, g_attn[None], g_pre[None], *gate_pieces, *up_pieces)


def ff_down(mixed, index, pieces, width):
    rows, ff = mixed.shape
    count = len(pieces)

    def body(index_ref, mix_ref, *refs):
        ins = refs[:count]
        f_ref, wd, sems = refs[count:]
        for copy in load_pieces(index_ref, ins, wd, sems):
            copy.wait()
        for at, size in spans(width, 384):
            f_ref[:, at : at + size] = dot_nt(wd[at : at + size, :], mix_ref[...]).T.astype(BF)

    return pl.pallas_call(
        body,
        out_shape=jax.ShapeDtypeStruct((rows, width), BF),
        in_specs=[smem(), vmem()] + [anywhere()] * count,
        out_specs=vmem(),
        scratch_shapes=[pltpu.VMEM((width, ff), BF), pltpu.SemaphoreType.DMA((count,))],
        compiler_params=PARAMS,
        name="ff_down",
    )(index, mixed, *pieces)


def ff_backward(f_sum, h1, cot, g_post, p1, p2, index, gate_pieces, up_pieces, down_pieces):
    rows, width = h1.shape
    ff = p1.shape[1]
    count = len(gate_pieces)

    def body(index_ref, f_ref, h1_ref, cot_ref, gp_ref, p1_ref, p2_ref, *refs):
        gates, ups, downs = refs[:count], refs[count : 2 * count], refs[2 * count : 3 * count]
        (out_ref, df_ref, gpost_ref, dg_ref, du_ref, dff_ref, wg, wu, wd, sem_g, sem_u, sem_d) = refs[
            3 * count :
        ]
        copies_d = load_pieces(index_ref, downs, wd, sem_d)
        copies = load_pieces(index_ref, gates, wg, sem_g)
        copies += load_pieces(index_ref, ups, wu, sem_u)
        f_hat, factor = rms_parts(f_ref[...].astype(F32))
        gain = gp_ref[...]
        out_ref[...] = h1_ref[...] + f_hat * gain
        up_stream = cot_ref[...].astype(F32)
        gpost_ref[...] = jnp.sum(up_stream * f_hat, axis=0, keepdims=True)
        df_ref[...] = rms_back(up_stream, f_hat, factor, gain).astype(BF)
        for copy in copies_d:
            copy.wait()

        def chunk(lanes):
            d_mixed = dot(df_ref[...], wd[:, lanes])
            dg_ref[:, lanes] = (d_mixed * p1_ref[:, lanes].astype(F32)).astype(BF)
            du_ref[:, lanes] = (d_mixed * p2_ref[:, lanes].astype(F32)).astype(BF)

        whole = ff // 256

        @pl.loop(0, whole)
        def _(c):
            chunk(pl.ds(pl.multiple_of(c * 256, 256), 256))

        if ff % 256:
            chunk(pl.ds(whole * 256, ff % 256))
        for copy in copies:
            copy.wait()
        for at, size in spans(width, 384):
            turned = dot_nt(wg[at : at + size, :], dg_ref[...]) + dot_nt(wu[at : at + size, :], du_ref[...])
            dff_ref[:, at : at + size] = turned.T.astype(BF)

    return pl.pallas_call(
        body,
        out_shape=(
            jax.ShapeDtypeStruct((rows, width), F32),
            jax.ShapeDtypeStruct((rows, width), BF),
            jax.ShapeDtypeStruct((1, width), F32),
            jax.ShapeDtypeStruct((rows, ff), BF),
            jax.ShapeDtypeStruct((rows, ff), BF),
            jax.ShapeDtypeStruct((rows, width), BF),
        ),
        in_specs=[smem()] + [vmem()] * 6 + [anywhere()] * (3 * count),
        out_specs=(vmem(),) * 6,
        scratch_shapes=[pltpu.VMEM((width, ff), BF)] * 3 + [pltpu.SemaphoreType.DMA((count,))] * 3,
        compiler_params=PARAMS,
        name="ff_backward",
    )(index, f_sum, h1, cot, g_post[None], p1, p2, *gate_pieces, *up_pieces, *down_pieces)


def weight_grads(index, groups):
    blocks = index.shape[0]
    half = blocks // 2
    rows, width = groups[0][0][0].shape
    size = width // blocks
    lefts, rights, plan = [], [], []
    for group in groups:
        at, places = 0, []
        for left, right in group:
            known = [i for i, seen in enumerate(lefts) if seen is left]
            if not known:
                lefts.append(left)
                known = [len(lefts) - 1]
            places.append((known[0], len(rights), at, right.shape[1]))
            rights.append(right)
            at += right.shape[1]
        plan.append((places, at))
    tiled = size % 16 == 0
    turned = lefts if tiled else [left.T.reshape(blocks, size, rows) for left in lefts]
    n_left, n_right, n_group = len(lefts), len(rights), len(groups)

    def body(index_ref, *refs):
        left_refs, right_refs = refs[:n_left], refs[n_left : n_left + n_right]
        outs = refs[n_left + n_right : n_left + n_right + 2 * n_group]
        held = refs[n_left + n_right + 2 * n_group : -n_group]
        sems = refs[-n_group:]

        def copy(g, side, j):
            block = half * side + j
            if tiled:
                start = pl.multiple_of(index_ref[block] * size, 16)
                source = held[g].at[pl.ds(start, size)]
            else:
                source = held[g].at[block]
            return pltpu.make_async_copy(source, outs[2 * g + side].at[j], sems[g].at[block])

        for g, (places, _) in enumerate(plan):
            if tiled:
                for li, ri, at, cols in places:
                    for row, step in spans(width, 384):
                        held[g][row : row + step, at : at + cols] = dot_tn(
                            left_refs[li][:, row : row + step], right_refs[ri][...]
                        ).astype(BF)
            else:

                @pl.loop(0, blocks)
                def _(j, g=g, places=places):
                    for li, ri, at, cols in places:
                        held[g][j, :, at : at + cols] = dot(
                            left_refs[li][index_ref[j]], right_refs[ri][...]
                        ).astype(BF)

            for side in (1, 0):
                for j in range(half):
                    copy(g, side, j).start()
        for g in range(n_group):
            for side in (1, 0):
                for j in range(half):
                    copy(g, side, j).wait()

    out_shape = []
    for _, cols in plan:
        out_shape += [jax.ShapeDtypeStruct((half, size, cols), BF)] * 2
    outs = pl.pallas_call(
        body,
        out_shape=out_shape,
        in_specs=[smem()] + [vmem()] * (n_left + n_right),
        out_specs=[anywhere()] * (2 * n_group),
        scratch_shapes=[
            pltpu.VMEM((width, cols) if tiled else (blocks, size, cols), BF) for _, cols in plan
        ]
        + [pltpu.SemaphoreType.DMA((blocks,))] * n_group,
        compiler_params=PARAMS,
    )(index, *turned, *rights)
    return [(outs[2 * g], outs[2 * g + 1]) for g in range(n_group)]


def input_kernel(gathered, lead, quarter, wqkv, peers, peers_other, qc, d_resid, tokens, gain):
    rows, width = tokens.shape
    cols = wqkv.shape[1]
    kc = cols - qc
    n_tp = gathered.shape[0]
    order = xor_order(n_tp)
    count = len(peers)
    half = width // 2
    place = jnp.stack([lax.axis_index("shard"), lax.axis_index("tp")]).astype(jnp.int32)

    def body(place_ref, got_ref, own_ref, resid_ref, x_ref, gain_ref, *refs):
        mine, other = refs[:count], refs[count : 2 * count]
        out_ref, sum_ref, held, sem_a, sem_b = refs[2 * count :]
        shard, me = place_ref[0], place_ref[1]
        copies = []
        for refs_of, sems, side in ((mine, sem_a, shard), (other, sem_b, 1 - shard)):
            for i, ref in enumerate(refs_of):
                start = pl.multiple_of(side * half, 16)
                copy = pltpu.make_async_copy(ref, held.at[i, pl.ds(start, half)], sems.at[i])
                copy.start()
                copies.append(copy)

        def left(peer):
            lanes = pl.ds(pl.multiple_of(peer * kc, kc), kc)
            packed = got_ref[peer, :lead, :].reshape(rows // 2, 2 * qc)
            queries = jnp.concatenate([packed[:, :qc], packed[:, qc:]], axis=0)
            keys = jnp.concatenate(
                [got_ref[q, lead : lead + quarter, lanes] for q in range(n_tp)], axis=0
            )
            return jnp.concatenate([queries, keys], axis=1)

        total = dot_nt(left(me), own_ref[...])
        for copy in copies:
            copy.wait()
        for i in range(count):
            total = total + dot_nt(left(jnp.bitwise_xor(me, order[i + 1])), held[i])
        hat, factor = rms_parts(x_ref[...].astype(F32))
        sum_ref[...] = jnp.sum(total * hat, axis=0, keepdims=True)
        out_ref[...] = resid_ref[...] + rms_back(total, hat, factor, gain_ref[...])

    return pl.pallas_call(
        body,
        out_shape=(jax.ShapeDtypeStruct((rows, width), F32), jax.ShapeDtypeStruct((1, width), F32)),
        in_specs=[smem()] + [vmem()] * 5 + [anywhere()] * (2 * count),
        out_specs=(vmem(), vmem()),
        scratch_shapes=[
            pltpu.VMEM((count, width, cols), BF),
            pltpu.SemaphoreType.DMA((count,)),
            pltpu.SemaphoreType.DMA((count,)),
        ],
        compiler_params=PARAMS,
        name="input_kernel",
    )(place, gathered, wqkv, d_resid, tokens, gain[None], *peers, *peers_other)


def scatter_ctx(x):
    bits = bits_of(lax.axis_size("ctx"))
    for place, bit in enumerate(reversed(bits)):
        half = x.shape[0] // 2
        got = xor_swap(x[half:].astype(BF), "ctx", bit)
        x = x[:half].astype(F32) + got.astype(F32)
        if place + 1 < len(bits):
            x = x.astype(BF)
    return x


def scatter_pair(keep, send):
    parts = [keep, xor_swap(send, "shard", 1)]

    def total(first, last):
        return sum(part[first:last].astype(F32) for part in parts)

    end = keep.shape[0]
    for bit in reversed(bits_of(lax.axis_size("ctx"))):
        high = total(end // 2, end).astype(BF)
        parts.append(xor_swap(high, "ctx", bit))
        end = end // 2
    return total(0, 1)[0]


def scatter_split(keep, send):
    got = xor_swap(send, "shard", 1)
    sums = [[keep[i], got[i]] for i in range(keep.shape[0])]

    def total(parts):
        return sum(part.astype(F32) for part in parts)

    for bit in reversed(bits_of(lax.axis_size("ctx"))):
        half = len(sums) // 2
        for place in reversed(range(half, 2 * half)):
            block = total(sums[place]).astype(BF)
            sums[place - half].append(xor_swap(block, "ctx", bit))
        sums = sums[:half]
    return total(sums[0])


def all_reduce_tp(part):
    n = lax.axis_size("tp")
    rows = part.shape[0]
    sent = part.astype(BF).reshape((n, rows // n) + part.shape[1:])
    got = lax.all_to_all(sent, "tp", 0, 0)
    summed = jnp.sum(got.astype(F32), axis=0).astype(BF)
    return lax.all_gather(summed, "tp", axis=0, tiled=True)


def layer(
    inputs,
    positions,
    cotangent,
    w_query,
    w_keyval,
    w_out,
    w_gate,
    w_up,
    w_down,
    gain_input,
    gain_query,
    gain_key,
    gain_attn,
    gain_prefn,
    gain_postfn,
):
    tokens = inputs[0]
    cot = cotangent[0]
    tok_pos = positions[0]
    n_ctx = lax.axis_size("ctx")
    n_tp = lax.axis_size("tp")
    count, width = tokens.shape
    qc = w_query.shape[1]
    kc = w_keyval.shape[1]
    heads = qc // HD
    index = natural_index()
    rows = w_query.shape[0]

    group = 128
    cols = qc + kc + w_out.shape[1]
    starts = (tok_pos[::group] // group).astype(BF)
    tail = jnp.zeros((16, cols), BF).at[0, : count // group].set(starts)
    first = jnp.concatenate([jnp.concatenate([w_query, w_keyval, w_out], axis=1), tail], axis=0)
    first_mine = gather_direct(first)
    first_all = with_other_core(first_mine)
    block_starts = jnp.stack([p[rows, : count // group] for p in first_mine]).astype(jnp.int32)
    pos_all = (block_starts.reshape(-1, 1) * group + jnp.arange(group, dtype=jnp.int32)[None]).reshape(-1)
    if rows % 16:
        first_all = [p[:rows] for p in first_all]
    first_all = in_order(first_all, index)
    normed_in, qkv, wqkv, wo = qkv_kernel(tokens, gain_input, index, first_all, qc + kc)

    shard_rows = lax.dynamic_slice_in_dim(
        wqkv, lax.axis_index("shard") * (width // 2), width // 2, 0
    )
    tp_order = xor_order(n_tp)
    peers = [xor_swap(shard_rows, "tp", k) for k in tp_order[1:]]
    peers_other = [xor_swap(p, "shard", 1) for p in peers]

    cos_all, sin_all = rope_tables(pos_all)
    cosine, sine = cos_all[:count], sin_all[:count]
    q_raw = qkv[:, :qc].reshape(count, heads, HD)
    kv_part = qkv[:, qc:].astype(BF)

    kv_cols = jnp.concatenate(gather_direct(kv_part), axis=0)
    spread = jnp.broadcast_to(kv_cols[None], (n_tp,) + kv_cols.shape)
    kv_stack = lax.all_to_all(spread, "tp", 0, 0)
    kv_raw = jnp.concatenate([kv_stack[i] for i in range(n_tp)], axis=1)
    k_hat_all, k_factor_all = rms_parts(kv_raw[:, :HD].astype(F32))
    keys = rope(k_hat_all * gain_key, cos_all, sin_all).astype(BF)
    values = kv_raw[:, HD:]

    q_hat, q_factor = rms_parts(q_raw)
    queries = rope(q_hat * gain_query, cosine[:, None, :], sine[:, None, :]).astype(BF)
    visible = pos_all[None, :] <= tok_pos[:, None]

    scores, lses, outs = [], [], []
    for h in range(heads):
        s = dot_nt(queries[:, h], keys) * SCALE
        s = jnp.where(visible, s, -1e30)
        top = jnp.max(s, axis=-1, keepdims=True)
        w = jnp.exp(s - top)
        tot = jnp.sum(w, axis=-1, keepdims=True)
        outs.append((dot(w.astype(BF), values) / tot).astype(BF))
        lses.append(top + jnp.log(tot))
        scores.append(s)
    attn = jnp.concatenate(outs, axis=1)

    o_part = dot_nt(attn, wo).astype(BF)
    gate_mine = gather_doubling(w_gate, kv_cols)
    up_mine = gather_doubling(w_up, o_part)
    o_bf = all_reduce_tp(o_part)
    down_mine = gather_doubling(w_down, o_bf)
    gate_all = in_order(with_other_core([after(p, o_part) for p in gate_mine]), index)
    up_all = in_order(with_other_core([after(p, o_part) for p in up_mine[:-1]] + [after(up_mine[-1], o_bf)]), index)
    resid, normed_ff, mixed, p1, p2 = ff_forward(
        o_bf, tokens, gain_attn, gain_prefn, index, gate_all, up_all
    )
    down_all = in_order(with_other_core([after(p, o_bf) for p in down_mine]), index)
    f_bf = all_reduce_tp(ff_down(mixed, index, down_all, width))
    block_out, d_f, grad_postfn, d_gate, d_up, d_ff_part = ff_backward(
        f_bf, resid, cot, gain_postfn, p1, p2, index, gate_all, up_all, down_all
    )
    d_ff = all_reduce_tp(d_ff_part).astype(F32)
    (pair,) = weight_grads(index, [[(d_f, mixed)]])
    grad_down = scatter_split(*pair)
    (pair,) = weight_grads(index, [[(normed_ff, d_gate)]])
    grad_gate = scatter_split(*pair)
    (pair,) = weight_grads(index, [[(after(normed_ff, d_ff), d_up)]])
    grad_up = scatter_split(*pair)

    o_hat, o_factor = rms_parts(o_bf.astype(F32))
    h_hat, h_factor = rms_parts(resid)
    upstream = cot.astype(F32)
    grad_prefn = jnp.sum(d_ff * h_hat, axis=0)
    d_resid = upstream + rms_back(d_ff, h_hat, h_factor, gain_prefn)
    grad_attn = jnp.sum(d_resid * o_hat, axis=0)
    d_o = rms_back(d_resid, o_hat, o_factor, gain_attn).astype(BF)
    d_attn = dot(d_o, wo).astype(BF)
    delta = jnp.sum(
        (d_attn.astype(F32) * attn.astype(F32)).reshape(count, heads, HD), axis=-1, keepdims=True
    )

    d_keys = jnp.zeros(keys.shape, F32)
    d_values = jnp.zeros(values.shape, F32)
    d_queries = []
    for h in range(heads):
        dah = d_attn[:, h * HD : (h + 1) * HD]
        probs = jnp.exp(scores[h] - lses[h])
        d_probs = dot_nt(dah, values)
        d_scores = (probs * (d_probs - delta[:, h])).astype(BF)
        d_queries.append(dot(d_scores, keys))
        d_keys = d_keys + dot_tn(d_scores, queries[:, h])
        d_values = d_values + dot_tn(probs.astype(BF), dah)

    quarter = count // n_tp
    dkv = jnp.concatenate([d_keys, d_values], axis=1).astype(BF)
    dkv = dkv.reshape(n_ctx, n_tp, quarter, 2 * HD).transpose(1, 0, 2, 3)
    dkv = lax.all_to_all(dkv, "tp", 0, 0)
    dkv = jnp.sum(dkv.astype(F32), axis=0).reshape(n_ctx * quarter, 2 * HD)
    dkv = scatter_ctx(dkv)
    at = lax.axis_index("tp") * quarter
    cos_q = lax.dynamic_slice_in_dim(cosine, at, quarter, 0)
    sin_q = lax.dynamic_slice_in_dim(sine, at, quarter, 0)
    khat_q = lax.dynamic_slice_in_dim(k_hat_all[:count], at, quarter, 0)
    kfac_q = lax.dynamic_slice_in_dim(k_factor_all[:count], at, quarter, 0)
    d_knorm = rope_back(dkv[:, :HD] * SCALE, cos_q, sin_q)
    grad_key_part = jnp.sum(d_knorm * khat_q, axis=0)
    d_kraw = rms_back(d_knorm, khat_q, kfac_q, gain_key)
    dkv_raw = jnp.concatenate([d_kraw, dkv[:, HD:]], axis=1).astype(BF)

    d_qnorm = rope_back(
        jnp.stack(d_queries, axis=1) * SCALE, cosine[:, None, :], sine[:, None, :]
    )
    grad_query_part = jnp.sum(d_qnorm * q_hat, axis=(0, 1))
    d_qraw = rms_back(d_qnorm, q_hat, q_factor, gain_query).astype(BF).reshape(count, qc)

    tail = jnp.concatenate([grad_query_part, grad_key_part])[None].astype(BF)
    tail = jnp.concatenate([tail, jnp.zeros((15, 2 * HD), BF)], axis=0)
    packed = jnp.concatenate([d_qraw[: count // 2], d_qraw[count // 2 :]], axis=1)
    packed = packed.reshape(-1, 2 * HD)
    lead = packed.shape[0]
    gathered = lax.all_gather(jnp.concatenate([packed, dkv_raw, tail], axis=0), "tp", axis=0)
    gain_sums = jnp.sum(gathered[:, lead + quarter].astype(F32), axis=0)
    at = lax.axis_index("tp") * kc
    dkv_cols = lax.dynamic_slice_in_dim(gathered[:, lead : lead + quarter], at, kc, 2).reshape(count, kc)
    d_qkv = jnp.concatenate([d_qraw, dkv_cols], axis=1)
    (pair,) = weight_grads(index, [[(normed_in, d_qkv), (d_o, attn)]])
    grad_heads = scatter_pair(*pair)
    input_grad, grad_input = input_kernel(
        gathered, lead, quarter, wqkv, peers, peers_other, qc, d_resid, tokens, gain_input
    )
    grad_input = grad_input[0]

    blocks = 2 * n_ctx
    wide = jnp.stack([grad_input, grad_attn, grad_prefn, grad_postfn[0]])
    both = jnp.concatenate(
        [
            wide.reshape(4, blocks, -1).transpose(1, 0, 2).reshape(blocks, -1),
            gain_sums.reshape(2, blocks, -1).transpose(1, 0, 2).reshape(blocks, -1),
        ],
        axis=1,
    )
    both = jnp.take(both, index, axis=0)[:, None]
    mine = scatter_pair(both[:n_ctx], both[n_ctx:].astype(BF))[0]
    small = HD // blocks
    size = width // blocks
    base = 4 * size
    return (
        block_out[None],
        input_grad[None],
        grad_heads[:, :qc],
        grad_heads[:, qc : qc + kc],
        grad_heads[:, qc + kc :],
        grad_gate,
        grad_up,
        grad_down,
        mine[:size],
        mine[base : base + small],
        mine[base + small :],
        mine[size : 2 * size],
        mine[2 * size : 3 * size],
        mine[3 * size : 4 * size],
    )


def solution(mesh):
    rows = P(("shard", "ctx"), "tp")
    tokens = P("shard", "ctx", None)
    gain = P(("shard", "ctx"))
    return jax.shard_map(
        layer,
        mesh=mesh,
        in_specs=(tokens, P("shard", "ctx"), tokens) + (rows,) * 6 + (P(),) * 6,
        out_specs=(tokens, tokens) + (rows,) * 6 + (gain,) * 6,
        check_vma=False,
    )
```
